256 devices in a mesh: row: 16 (over z, core), col: 16 (over x, y).
Axes of the slice: x: 4, y: 4, z: 8, core: 2. Of those that a mesh axis runs over, the one named last changes fastest.
Arguments:
- multipliers: float32 [256, 2, 16, 256], P(('row', 'col')), may hold values from -6 to 6
- residual: float32 [256, 2, 16, 256], P(('row', 'col')), may hold values from -18 to 18
- direction: float32 [256, 2, 16, 256], P(('row', 'col')), may hold values from -6 to 6
- energy_prev: float32 [16], replicated, may hold values from 262144 to 1048576
- hypersingular: bfloat16 [256, 1152, 1152], P(('row', 'col')), may hold values from -1 to 4, as said below
- double_layer: bfloat16 [256, 1152, 1152], P(('row', 'col')), may hold values from -0.1875 to 0.1875
- single_inverse: bfloat16 [256, 1152, 1152], P(('row', 'col')), may hold values from -1 to 4, as said below
- neumann_inverse: bfloat16 [256, 1152, 1152], P(('row', 'col')), may hold values from -1 to 4, as said below
- rigid_modes: float32 [256, 6, 1152], P(('row', 'col')), may hold values from -0.75 to 0.75
- coarse_inverse: float32 [1536, 1536], P(('row', 'col')), may hold values from -0.625 to 0.625
- face_index: int32 [256, 4, 256], P(('row', 'col')), may hold values from 0 to 1151, as said below
Outputs:
- multipliers_next: float32 [256, 2, 16, 256], P(('row', 'col'))
- residual_next: float32 [256, 2, 16, 256], P(('row', 'col'))
- direction_next: float32 [256, 2, 16, 256], P(('row', 'col'))
The draws below stay inside these ranges and needn't reach their ends.
Inputs may be any that keep to these rules, and one draw needn't show every extreme that they name: For each patch the 1024 entries of face_index are distinct. `hypersingular`: each patch's matrix is symmetric positive definite. `single_inverse`: each patch's matrix is symmetric positive definite. `neumann_inverse`: each patch's matrix is symmetric positive definite.
All inputs are finite; a program needn't handle non-finite values.
Results may differ from the reference program's by a relative error of at most 0.0015.
Values sent between devices are 32-bit elements; how exact they have to be, the bound alone decides.
No kernel may reach another device: no remote copies, remote signals or barrier semaphores. Data moves between devices by JAX's collectives and lax.ppermute only.
A program may use at most 64 MiB of HBM per device.

```python
import math
import jax
import jax.numpy as jnp
from jax import lax

NB = 1152
IF = 256
NRHS = 16
RM = 6
ITERS = 1
PATCHES = 256
N_ROW = 16
N_COL = 16


def symmetric_block(key):

    def one_patch(patch_index):
        sub_key = jax.random.fold_in(key, patch_index)
        key_pair = jax.random.split(sub_key, 2)
        diagonal = jax.random.uniform(key_pair[0], (NB,), jnp.float32, 1.2, 3.0)
        off_diagonal = jnp.clip(jax.random.normal(key_pair[1], (NB, NB), jnp.float32), -4.0, 4.0)
        off_diagonal = (off_diagonal + off_diagonal.T) * (0.4 / jnp.sqrt(2.0 * NB))
        return off_diagonal + jnp.diag(diagonal)
    return lax.map(one_patch, jnp.arange(PATCHES))


def draw_hypersingular(key, part):
    return symmetric_block(jax.random.fold_in(key, 101)).astype(jnp.bfloat16)


def draw_single_inverse(key, part):
    return symmetric_block(jax.random.fold_in(key, 202)).astype(jnp.bfloat16)


def draw_neumann_inverse(key, part):
    return symmetric_block(jax.random.fold_in(key, 303)).astype(jnp.bfloat16)


def draw_residual(key, part):
    key_set = jax.random.split(jax.random.fold_in(key, 404), 1)
    rising = 1.0 + 2.0 * jnp.arange(PATCHES, dtype=jnp.float32) / max(PATCHES - 1, 1)
    shape_all = (PATCHES, 2, NRHS, IF)
    base_draw = jnp.clip(jax.random.normal(key_set[0], shape_all, jnp.float32), -6.0, 6.0)
    return jnp.clip(base_draw * rising[:, None, None, None], -18.0, 18.0)


def draw_face_index(key, part):

    def one_patch(patch_index):
        shuffled = jax.random.permutation(jax.random.fold_in(key, patch_index), NB)
        return shuffled[:4 * IF].reshape(4, IF).astype(jnp.int32)
    return lax.map(one_patch, jnp.arange(PATCHES))


def with_spikes(array, key, source, target, shards_of, factor):
    def block_of(dim):
        return (jnp.arange(array.shape[dim]) // (array.shape[dim] // shards_of)).reshape((-1,) + (1,) * (array.ndim - 1 - dim))

    near = jax.random.permutation(key, shards_of)[block_of(target)]
    other_side = (block_of(target) + shards_of // 2) % shards_of
    return jnp.where((block_of(source) == near) | (block_of(source) == other_side), factor * array, array)


def block_scale(stream_key, extent, cuts, least, high):
    gain = 1.0
    for axis_at, parts in cuts:
        draws = jax.random.uniform(jax.random.fold_in(jax.random.fold_in(stream_key, 6), axis_at), (parts,), jnp.float32, least / len(cuts), high / len(cuts))
        gain = gain * jnp.repeat(jnp.exp(draws), extent[axis_at] // parts).reshape((-1,) + (1,) * (len(extent) - 1 - axis_at))
    return gain


def gaussian(stream_key, extent, scale, bound, shards=(), kind=jnp.bfloat16):
    drawn = scale * jax.random.normal(stream_key, extent, jnp.float32)
    if shards:
        drawn = drawn * block_scale(stream_key, extent, shards, -0.22, 0.18)
    return jnp.clip(drawn, -bound, bound).astype(kind)


def gaussian_with(own_key, dims, scale, reach, shards, heavy, kind=jnp.bfloat16):
    result = scale * jax.random.normal(own_key, dims, jnp.float32)
    if shards:
        result = result * block_scale(own_key, dims, shards, -0.22, 0.18)
    return jnp.clip(with_spikes(result, jax.random.fold_in(own_key, 3), *heavy), -reach, reach).astype(kind)


def setup_inputs(seed: int = 0) -> dict:
    arg_keys = jax.random.split(jax.random.key(seed), 12)
    multipliers = gaussian(arg_keys[0], (PATCHES, 2, NRHS, IF), 1.0, 6.0, ((0, 256),), jnp.float32)
    residual = draw_residual(jax.random.fold_in(arg_keys[11], 71), 0)
    direction = gaussian(arg_keys[2], (PATCHES, 2, NRHS, IF), 1.0, 6.0, ((0, 256),), jnp.float32)
    energy_prev = jnp.clip(jnp.exp(jax.random.uniform(arg_keys[3], (NRHS,), jnp.float32, math.log(262144.0), math.log(1048576))), 262144.0, 1048576)
    hypersingular = draw_hypersingular(jax.random.fold_in(arg_keys[11], 71), 0)
    double_layer = gaussian(arg_keys[5], (PATCHES, NB, NB), NB ** -0.5, 0.1875, ((0, 256),))
    single_inverse = draw_single_inverse(jax.random.fold_in(arg_keys[11], 71), 0)
    neumann_inverse = draw_neumann_inverse(jax.random.fold_in(arg_keys[11], 71), 0)
    rigid_modes = gaussian(arg_keys[8], (PATCHES, RM, NB), 64 ** -0.5, 0.75, ((0, 256),), jnp.float32)
    coarse_inverse = gaussian_with(arg_keys[9], (PATCHES * RM, PATCHES * RM), (PATCHES * RM) ** -0.5, 0.625, ((0, 256),), (1, 0, 256, 6.0), jnp.float32)
    face_index = draw_face_index(jax.random.fold_in(arg_keys[11], 71), 0)
    return dict(multipliers=multipliers, residual=residual, direction=direction, energy_prev=energy_prev, hypersingular=hypersingular, double_layer=double_layer, single_inverse=single_inverse, neumann_inverse=neumann_inverse, rigid_modes=rigid_modes, coarse_inverse=coarse_inverse, face_index=face_index)


highest = lax.Precision.HIGHEST


def rolled(vectors, row_step, col_step):
    shaped = vectors.reshape((N_ROW, N_COL) + vectors.shape[1:])
    shaped = jnp.roll(shaped, (row_step, col_step), axis=(0, 1))
    return shaped.reshape(vectors.shape)


def spread_faces(values, face_index):
    from_left = rolled(values[:, 0], 0, 1)
    from_below = rolled(values[:, 1], 1, 0)
    pieces = jnp.concatenate([values[:, 0], values[:, 1], -from_left, -from_below], axis=2)
    flat_index = face_index.reshape(face_index.shape[0], -1)

    def place_one(piece_row, where_row):
        return jnp.zeros((piece_row.shape[0], NB), jnp.float32).at[:, where_row].set(piece_row)

    return jax.vmap(place_one)(pieces, flat_index)


def jump_faces(vectors, face_index):
    flat_index = face_index.reshape(face_index.shape[0], -1)

    def pick_one(row_vec, where_row):
        return jnp.take(row_vec, where_row, axis=1)

    picked = jax.vmap(pick_one)(vectors, flat_index)
    face_width = face_index.shape[2]
    own_right = picked[:, :, :face_width]
    own_upper = picked[:, :, face_width:2 * face_width]
    side_left = picked[:, :, 2 * face_width:3 * face_width]
    side_lower = picked[:, :, 3 * face_width:]
    return jnp.stack([own_right - rolled(side_left, 0, -1), own_upper - rolled(side_lower, -1, 0)], axis=1)


def project(values, face_index, rigid_modes, coarse_inverse):
    spread = spread_faces(values, face_index)
    partial_value = jnp.einsum("pmn,pkn->pmk", rigid_modes, spread, precision=highest)
    stacked = partial_value.reshape(-1, partial_value.shape[2])
    coarse_coef = jnp.dot(coarse_inverse, stacked, precision=highest).reshape(partial_value.shape)
    modes_back = jnp.einsum("pmk,pmn->pkn", coarse_coef, rigid_modes, precision=highest)
    return values - jump_faces(modes_back, face_index)


def dirichlet_patch(operands):
    spread, hypersingular, double_layer, single_inverse = operands
    rounded = spread.astype(jnp.bfloat16)
    lifted = (0.5 * rounded.astype(jnp.float32) + jnp.dot(rounded, double_layer, preferred_element_type=jnp.float32)).astype(jnp.bfloat16)
    weighed = jnp.dot(lifted, single_inverse, preferred_element_type=jnp.float32).astype(jnp.bfloat16)
    applied = jnp.dot(rounded, hypersingular, preferred_element_type=jnp.float32) + 0.5 * weighed.astype(jnp.float32) + lax.dot_general(weighed, double_layer, (((1,), (1,)), ((), ())), preferred_element_type=jnp.float32)
    energy = jnp.sum(rounded.astype(jnp.float32) * applied, axis=1)
    return applied, energy


def neumann_patch(operands):
    rounded, neumann_inverse = operands
    return jnp.dot(rounded, neumann_inverse, preferred_element_type=jnp.float32)


def reference(multipliers, residual, direction, energy_prev, hypersingular, double_layer, single_inverse, neumann_inverse, rigid_modes, coarse_inverse, face_index):
    cases = residual.shape[2]
    for iteration in range(ITERS):
        projected = project(residual, face_index, rigid_modes, coarse_inverse)
        spread_now = spread_faces(projected, face_index)
        applied, energy_parts = lax.map(dirichlet_patch, (spread_now, hypersingular, double_layer, single_inverse))
        energy = jnp.sum(energy_parts, axis=0)
        searched = project(jump_faces(applied, face_index), face_index, rigid_modes, coarse_inverse)
        paired = spread_faces(jnp.concatenate([searched, direction], axis=2), face_index).astype(jnp.bfloat16)
        paired_applied = lax.map(neumann_patch, (paired, neumann_inverse))
        step_ratio = energy / energy_prev
        ratio_col = step_ratio[None, :, None]
        spread_dir = paired[:, :cases].astype(jnp.float32) + ratio_col * paired[:, cases:].astype(jnp.float32)
        applied_dir = paired_applied[:, :cases] + ratio_col * paired_applied[:, cases:]
        curvature = jnp.sum(spread_dir * applied_dir, axis=(0, 2))
        step_size = energy / curvature
        direction = searched + step_ratio[None, None, :, None] * direction
        multipliers = multipliers + step_size[None, None, :, None] * direction
        corrected = project(jump_faces(applied_dir, face_index), face_index, rigid_modes, coarse_inverse)
        residual = residual - step_size[None, None, :, None] * corrected
        energy_prev = energy
    return multipliers, residual, direction
```

```python
import jax
import jax.numpy as jnp
from jax import lax
from jax.experimental import pallas as pl
from jax.experimental.pallas import tpu as pltpu
from jax.sharding import PartitionSpec as P


NB = 1152
IF = 256
NF = 4 * IF
K = 16
RM = 6
GROUP = 32
SUMS = 31
LANES = 128
f32 = jnp.float32
bf16 = jnp.bfloat16
highest = lax.Precision.HIGHEST
contract_last = (((1,), (1,)), ((), ()))
VMEM = pl.BlockSpec(memory_space=pltpu.VMEM)
ANY = pl.BlockSpec(memory_space=pl.ANY)


def exact_dot(a, b):
    return jnp.dot(a, b, precision=highest, preferred_element_type=f32)


def exact_dot_nt(a, b):
    return lax.dot_general(a, b, contract_last, precision=highest, preferred_element_type=f32)


def bf_dot(a, b):
    return jnp.dot(a, b, preferred_element_type=f32)


def bf_dot_nt(a, b):
    return lax.dot_general(a, b, contract_last, preferred_element_type=f32)


def thirds(x):
    high = x.astype(bf16).astype(f32)
    rest = x - high
    middle = rest.astype(bf16).astype(f32)
    return jnp.concatenate([high, middle, rest - middle], axis=0).astype(bf16)


def one_hot(face_ref, a):
    where = face_ref[a : a + 1, :]
    rows = lax.broadcasted_iota(jnp.int32, (NB, IF), 0)
    return jnp.where(rows == where, 1.0, 0.0).astype(bf16)


def build_places(face_ref, place):
    for a in range(4):
        place[:, a * IF : (a + 1) * IF] = one_hot(face_ref, a)


def fold_matrix():
    case = lax.broadcasted_iota(jnp.int32, (K, LANES), 0)
    lane = lax.broadcasted_iota(jnp.int32, (K, LANES), 1)
    return jnp.where((lane & (K - 1)) == case, 1.0, 0.0).astype(f32)


def sum_row(prod):
    row = lax.broadcasted_iota(jnp.int32, (8, prod.shape[1]), 0)
    pick = jnp.where(row == RM, 1.0, 0.0).astype(f32)
    return exact_dot_nt(pick, prod)


def payload(terms):
    spread_out = exact_dot(terms, fold_matrix())
    row = lax.broadcasted_iota(jnp.int32, (8, LANES), 0)
    lane = lax.broadcasted_iota(jnp.int32, (8, LANES), 1)
    flat = jnp.sum(jnp.where((lane >> 4) == row, spread_out, 0.0), axis=0, keepdims=True)
    return jnp.broadcast_to(flat, (K, LANES))


def coefficients(gathered, coarse):
    terms = exact_dot(coarse, gathered)
    lane = lax.broadcasted_iota(jnp.int32, (GROUP, LANES), 1)
    total = jnp.zeros((GROUP, LANES), f32)
    for m in range(RM + 1):
        total = total + jnp.where((lane >> 4) == m, terms[m * GROUP : (m + 1) * GROUP], 0.0)
    return exact_dot_nt(fold_matrix(), total)


def prepare_kernel(face_ref, modes_ref, coarse_ref, dir_ref, rf_ref, right_ref, upper_ref, left_ref, lower_ref):
    modes = jnp.concatenate([modes_ref[...], jnp.zeros((8 - RM, NB), f32)], axis=0)
    parts = thirds(modes)
    for a, message in enumerate((right_ref, upper_ref, left_ref, lower_ref)):
        picked = bf_dot(parts, one_hot(face_ref, a))
        rf = picked[:8] + picked[8:16] + picked[16:24]
        rf_ref[:, a * IF : (a + 1) * IF] = rf
        message[0:36, :] = coarse_ref[...]
        message[36:40, :] = jnp.zeros((4, IF), f32)
        message[40:48, :] = rf
        if a < 2:
            message[48:64, :] = dir_ref[a]


def first_kernel(res_ref, from_left_ref, from_below_ref, rf_ref, w_ref, pay_ref):
    w = jnp.concatenate([res_ref[0], res_ref[1], -from_left_ref[...], -from_below_ref[...]], axis=1)
    w_ref[...] = w
    pay_ref[...] = payload(exact_dot_nt(rf_ref[...], w))


def swap_kernel(p0, p1, p2, p3, q0, q1, q2, q3, rf_ref, sums_ref, w_ref, pay_ref):
    own = jnp.concatenate([p0[...], p1[...], p2[...], p3[...]], axis=1)
    other = jnp.concatenate([q0[...], q1[...], q2[...], q3[...]], axis=1)
    w = own - other
    w_ref[...] = w
    pay_ref[...] = payload(exact_dot_nt(rf_ref[...], w) + sums_ref[...])


def store_faces(vectors, place, faces):
    picked = bf_dot(thirds(vectors), place[...])
    picked = picked[:K] + picked[K : 2 * K] + picked[2 * K :]
    for a, face in enumerate(faces):
        face[...] = picked[:, a * IF : (a + 1) * IF]


def dirichlet_kernel(
    gathered_ref, coarse_ref, rf_ref, right_ref, upper_ref, left_ref, lower_ref, w_ref, face_ref,
    double_hbm, single_hbm, hyper_hbm,
    big_ref, modes_ref, p0, p1, p2, p3, sums_ref,
    double, single, hyper, place, sems,
):
    copies = [
        pltpu.make_async_copy(src.at[0], dst, sems.at[i])
        for i, (src, dst) in enumerate(((double_hbm, double), (single_hbm, single), (hyper_hbm, hyper)))
    ]
    for copy in copies:
        copy.start()
    build_places(face_ref, place)
    big_ref[...] = jnp.zeros_like(big_ref)
    modes_ref[...] = jnp.zeros_like(modes_ref)
    for p, src in enumerate((coarse_ref, right_ref, upper_ref, left_ref, lower_ref)):
        for m in range(RM):
            at = m * GROUP + p * RM
            big_ref[at : at + RM, :] = src[m * RM : (m + 1) * RM, :]
        if p == 0:
            modes_ref[0:RM, :] = -rf_ref[0:RM, :]
        else:
            modes_ref[p * RM : (p + 1) * RM, (p - 1) * IF : p * IF] = src[40 : 40 + RM, :]
    big_ref[RM * GROUP + SUMS : RM * GROUP + SUMS + 1, :] = jnp.ones((1, IF), f32)
    coef = coefficients(gathered_ref[...], big_ref[...])
    w = w_ref[...] + exact_dot(coef, modes_ref[...])
    rounded = bf_dot_nt(w.astype(bf16), place[...])
    rounded_low = rounded.astype(bf16)
    copies[0].wait()
    lifted = (0.5 * rounded + bf_dot(rounded_low, double[...])).astype(bf16)
    copies[1].wait()
    weighed = bf_dot(lifted, single[...]).astype(bf16)
    applied = 0.5 * weighed.astype(f32) + bf_dot_nt(weighed, double[...])
    copies[2].wait()
    applied = applied + bf_dot(rounded_low, hyper[...])
    store_faces(applied, place, (p0, p1, p2, p3))
    sums_ref[...] = sum_row(rounded * applied)


def neumann_kernel(
    gathered_ref, big_ref, modes_ref, w_ref, dir_ref, left_ref, lower_ref, prev_ref, face_ref, neumann_hbm,
    p0, p1, p2, p3, sums_ref, next_ref, energy_ref,
    neumann, place, sems,
):
    copy = pltpu.make_async_copy(neumann_hbm.at[0], neumann, sems.at[0])
    copy.start()
    build_places(face_ref, place)
    coef = coefficients(gathered_ref[...], big_ref[...])
    energy = coef[:, SUMS : SUMS + 1]
    eye = lax.broadcasted_iota(jnp.int32, (K, K), 0) == lax.broadcasted_iota(jnp.int32, (K, K), 1)
    prev = jnp.sum(jnp.where(eye, jnp.broadcast_to(prev_ref[...], (K, K)), 0.0), axis=1, keepdims=True)
    ratio = energy / prev
    searched = w_ref[...] + exact_dot(coef, modes_ref[...])
    direction = jnp.concatenate(
        [dir_ref[0], dir_ref[1], -left_ref[48:64, :], -lower_ref[48:64, :]], axis=1
    )
    both = jnp.concatenate([searched, direction], axis=0).astype(bf16)
    paired = bf_dot_nt(both, place[...])
    spread_dir = paired[:K] + ratio * paired[K:]
    for s in range(2):
        next_ref[s] = searched[:, s * IF : (s + 1) * IF] + ratio * dir_ref[s]
    energy_ref[...] = jnp.broadcast_to(energy, (K, LANES))
    copy.wait()
    paired_applied = bf_dot(paired.astype(bf16), neumann[...])
    applied_dir = paired_applied[:K] + ratio * paired_applied[K:]
    store_faces(applied_dir, place, (p0, p1, p2, p3))
    sums_ref[...] = sum_row(spread_dir * applied_dir)


def last_kernel(
    gathered_ref, big_ref, modes_ref, w_ref, mult_ref, res_ref, next_ref, energy_ref,
    mult_out, res_out,
):
    coef = coefficients(gathered_ref[...], big_ref[...])
    step = energy_ref[:, 0:1] / coef[:, SUMS : SUMS + 1]
    corrected = w_ref[:, : 2 * IF] + exact_dot(coef, modes_ref[:, : 2 * IF])
    for s in range(2):
        mult_out[s] = mult_ref[s] + step * next_ref[s]
        res_out[s] = res_ref[s] - step * corrected[:, s * IF : (s + 1) * IF]


def call(kernel, outs, args, specs=None, scratch=()):
    return pl.pallas_call(
        kernel,
        out_shape=[jax.ShapeDtypeStruct(s, f32) for s in outs],
        in_specs=specs or [VMEM] * len(args),
        out_specs=[VMEM] * len(outs),
        scratch_shapes=list(scratch),
        compiler_params=pltpu.CompilerParams(vmem_limit_bytes=24 * 2**20),
        name=kernel.__name__,
    )(*args)


def shifted(block, axis, distance):
    devices = range(lax.axis_size(axis))
    route = [((i - distance) % len(devices), i) for i in devices]
    return lax.ppermute(block, axis, route)


def gather_all(rows):
    column = lax.all_to_all(rows.reshape(K, 1, LANES), "row", 0, 0)
    copies = jnp.broadcast_to(column.reshape(1, K, LANES), (K, K, LANES))
    return lax.all_to_all(copies, "col", 0, 0).reshape(K * K, LANES)


def swapped(faces):
    return (
        shifted(faces[2], "col", -1),
        shifted(faces[3], "row", -1),
        shifted(faces[0], "col", 1),
        shifted(faces[1], "row", 1),
    )


def on_device(
    multipliers, residual, direction, energy_prev, hypersingular, double_layer, single_inverse,
    neumann_inverse, rigid_modes, coarse_inverse, face_index,
):
    res, mult, dirs = residual[0], multipliers[0], direction[0]
    faces = face_index[0]
    res_left = shifted(res[0], "col", 1)
    res_below = shifted(res[1], "row", 1)
    coarse = coarse_inverse.reshape(RM, 16, 16, RM).transpose(3, 0, 2, 1).reshape(RM * RM, 256)
    rf, to_right, to_upper, to_left, to_lower = call(
        prepare_kernel,
        [(8, NF), (64, IF), (64, IF), (48, IF), (48, IF)],
        (faces, rigid_modes[0], coarse, dirs),
    )
    from_left = shifted(to_right, "col", 1)
    from_below = shifted(to_upper, "row", 1)
    from_right = shifted(to_left, "col", -1)
    from_above = shifted(to_lower, "row", -1)
    w, pay = call(first_kernel, [(K, NF), (K, LANES)], (res, res_left, res_below, rf))
    big, modes, *own, sums = call(
        dirichlet_kernel,
        [((RM + 1) * GROUP, IF), (GROUP, NF)] + [(K, IF)] * 4 + [(8, K)],
        (
            gather_all(pay), coarse, rf, from_right, from_above, from_left, from_below, w, faces,
            double_layer, single_inverse, hypersingular,
        ),
        [VMEM] * 9 + [ANY] * 3,
        [pltpu.VMEM((NB, NB), bf16)] * 3 + [pltpu.VMEM((NB, NF), bf16), pltpu.SemaphoreType.DMA((3,))],
    )
    w, pay = call(swap_kernel, [(K, NF), (K, LANES)], (*own, *swapped(own), rf, sums))
    *own, sums, dir_next, energy = call(
        neumann_kernel,
        [(K, IF)] * 4 + [(8, K), (2, K, IF), (K, LANES)],
        (
            gather_all(pay), big, modes, w, dirs, from_left, from_below, energy_prev.reshape(1, K), faces,
            neumann_inverse,
        ),
        [VMEM] * 9 + [ANY],
        [pltpu.VMEM((NB, NB), bf16), pltpu.VMEM((NB, NF), bf16), pltpu.SemaphoreType.DMA((1,))],
    )
    w, pay = call(swap_kernel, [(K, NF), (K, LANES)], (*own, *swapped(own), rf, sums))
    mult_next, res_next = call(
        last_kernel,
        [(2, K, IF)] * 2,
        (gather_all(pay), big, modes, w, mult, res, dir_next, energy),
    )
    return mult_next[None], res_next[None], dir_next[None]


def solution(mesh):
    whole = P(("row", "col"), None, None, None)
    patch = P(("row", "col"), None, None)
    return jax.shard_map(
        on_device,
        mesh=mesh,
        in_specs=(whole, whole, whole, P(), patch, patch, patch, patch, patch, P(("row", "col"), None), patch),
        out_specs=(whole, whole, whole),
        check_vma=False,
    )
```

```python
import jax
import jax.numpy as jnp
from jax import lax
from jax.experimental import pallas as pl
from jax.experimental.pallas import tpu as pltpu
from jax.sharding import PartitionSpec as P


NB = 1152
IF = 256
NF = 4 * IF
K = 16
RM = 6
GROUP = 32
SUMS = 31
CELLS = 64
LANES = 128
f32 = jnp.float32
bf16 = jnp.bfloat16
highest = lax.Precision.HIGHEST
contract_last = (((1,), (1,)), ((), ()))
VMEM = pl.BlockSpec(memory_space=pltpu.VMEM)
HBM = pl.BlockSpec(memory_space=pltpu.HBM)


def exact_dot(a, b):
    return jnp.dot(a, b, precision=highest, preferred_element_type=f32)


def exact_dot_nt(a, b):
    return lax.dot_general(a, b, contract_last, precision=highest, preferred_element_type=f32)


def bf_dot(a, b):
    return jnp.dot(a, b, preferred_element_type=f32)


def bf_dot_nt(a, b):
    return lax.dot_general(a, b, contract_last, preferred_element_type=f32)


def thirds(x):
    high = x.astype(bf16).astype(f32)
    rest = x - high
    middle = rest.astype(bf16).astype(f32)
    return jnp.concatenate([high, middle, rest - middle], axis=0).astype(bf16)


def one_hot(face_ref, a):
    where = face_ref[a : a + 1, :]
    rows = lax.broadcasted_iota(jnp.int32, (NB, IF), 0)
    return jnp.where(rows == where, 1.0, 0.0).astype(bf16)


def build_places(face_ref, place):
    for a in range(4):
        place[:, a * IF : (a + 1) * IF] = one_hot(face_ref, a)


def fold_matrix():
    case = lax.broadcasted_iota(jnp.int32, (K, LANES), 0)
    lane = lax.broadcasted_iota(jnp.int32, (K, LANES), 1)
    return jnp.where((lane & (K - 1)) == case, 1.0, 0.0).astype(f32)


def sum_row(prod):
    row = lax.broadcasted_iota(jnp.int32, (8, prod.shape[1]), 0)
    sums = exact_dot_nt(jnp.where(row == 7, 1.0, 0.0).astype(f32), prod)
    return jnp.concatenate([jnp.zeros((GROUP - 8, K), f32), sums], axis=0)


def flattened(terms):
    rows = terms.shape[0]
    spread_out = exact_dot(terms, fold_matrix())
    row = lax.broadcasted_iota(jnp.int32, (rows, LANES), 0)
    lane = lax.broadcasted_iota(jnp.int32, (rows, LANES), 1)
    kept = jnp.where((lane >> 4) == (row & 7), spread_out, 0.0)
    return jnp.sum(kept.reshape(rows // 8, 8, LANES), axis=1)


def copied(row_block, ref):
    ref[...] = jnp.broadcast_to(row_block[None], (ref.shape[0] // 8, 8, LANES)).reshape(ref.shape)


def fold_terms(terms, blocks, total):
    lane = lax.broadcasted_iota(jnp.int32, (GROUP, LANES), 1)
    for m in range(blocks):
        total = total + jnp.where((lane >> 4) == m, terms[m * GROUP : (m + 1) * GROUP], 0.0)
    return total


def first_coefficients(gathered_ref, coarse_ref):
    terms = exact_dot(coarse_ref[: RM * GROUP], gathered_ref[...])
    return exact_dot_nt(fold_matrix(), fold_terms(terms, RM, jnp.zeros((GROUP, LANES), f32)))


def coefficients(gathered_ref, coarse_ref):
    total = jnp.zeros((GROUP, LANES), f32)
    for q in range(4):
        lanes = gathered_ref[pl.ds(q, 256, stride=4), :]
        total = fold_terms(exact_dot(coarse_ref[q * 256 : (q + 1) * 256], lanes), 8, total)
    return exact_dot_nt(fold_matrix(), total)


def neighbour_payload(modes_ref, faces, sums, pay_ref):
    terms = sums - exact_dot_nt(modes_ref[...], faces)
    flat = flattened(terms)
    copied(jnp.concatenate([flat, flat], axis=0), pay_ref)


def start_all(pairs, sems):
    copies = [pltpu.make_async_copy(src, dst, sems.at[i]) for i, (src, dst) in enumerate(pairs)]
    for copy in copies:
        copy.start()
    return copies


def coarse_by_mode(coarse):
    width = CELLS * RM
    rows = jnp.concatenate([coarse[:, c * width : (c + 1) * width] for c in range(4)], axis=0)
    source = lax.broadcasted_iota(jnp.int32, (width, width), 0)
    target = lax.broadcasted_iota(jnp.int32, (width, width), 1)
    wanted = (target & (CELLS - 1)) * RM + (target >> 6)
    sorting = jnp.where(source == wanted, 1.0, 0.0).astype(bf16)
    moved = bf_dot(thirds(rows), sorting)
    moved = moved[: 4 * RM] + moved[4 * RM : 8 * RM] + moved[8 * RM :]
    return [
        jnp.concatenate(
            [moved[c * RM : (c + 1) * RM, m * CELLS : (m + 1) * CELLS] for c in range(4)], axis=1
        )
        for m in range(RM)
    ]


def prepare_kernel(
    face_hbm, modes_hbm, coarse_hbm, dir_hbm,
    rf_ref, faces_ref, right_ref, upper_ref, left_ref, lower_ref,
    modes_in, coarse_in, dir_in, sems,
):
    copies = start_all(
        ((face_hbm, faces_ref), (modes_hbm, modes_in), (coarse_hbm, coarse_in), (dir_hbm, dir_in)), sems
    )
    for copy in copies:
        copy.wait()
    modes = jnp.concatenate([modes_in[...], jnp.zeros((8 - RM, NB), f32)], axis=0)
    parts = thirds(modes)
    sorted_rows = coarse_by_mode(coarse_in[...])
    for a, message in enumerate((right_ref, upper_ref, left_ref, lower_ref)):
        picked = bf_dot(parts, one_hot(faces_ref, a))
        rf = picked[:8] + picked[8:16] + picked[16:24]
        rf_ref[:, a * IF : (a + 1) * IF] = rf
        for m in range(RM):
            message[m * RM : (m + 1) * RM, :] = sorted_rows[m]
        message[36:40, :] = jnp.zeros((4, IF), f32)
        message[40:48, :] = rf
        message[48:64, :] = dir_in[a & 1]


def first_kernel(res_hbm, from_left_ref, from_below_ref, rf_ref, w_ref, pay_ref, res, sems):
    (copy,) = start_all(((res_hbm, res),), sems)
    copy.wait()
    w = jnp.concatenate([res[0], res[1], -from_left_ref[0], -from_below_ref[1]], axis=1)
    w_ref[...] = w
    flat = flattened(exact_dot_nt(rf_ref[...], w))
    copied(jnp.broadcast_to(flat, (8, LANES)), pay_ref)


def moved_to(rows, p):
    lane = lax.broadcasted_iota(jnp.int32, rows.shape, 1) & 15
    if p == 0:
        return rows
    if p == 1:
        return jnp.where(lane == 15, pltpu.roll(rows, 15, 1), pltpu.roll(rows, 255, 1))
    if p == 2:
        return pltpu.roll(rows, 240, 1)
    if p == 3:
        return jnp.where(lane == 0, pltpu.roll(rows, 241, 1), pltpu.roll(rows, 1, 1))
    return pltpu.roll(rows, 16, 1)


def assemble_kernel(
    own_right, own_upper, rf_ref, right_ref, upper_ref, left_ref, lower_ref, big_ref, modes_ref, dir_ref
):
    big_ref[...] = jnp.zeros_like(big_ref)
    modes_ref[...] = jnp.zeros_like(modes_ref)
    modes_ref[0:RM, :] = -rf_ref[0:RM, :]
    for holder, src in enumerate((own_right, right_ref, upper_ref, left_ref, lower_ref)):
        rows = src[0:40, :]
        for p in range(5):
            moved = moved_to(rows, p)
            for m in range(RM):
                at = (p * RM + m) * GROUP + holder * RM
                big_ref[at : at + RM, :] = moved[m * RM : (m + 1) * RM, :]
        if holder:
            part = slice((holder - 1) * IF, holder * IF)
            modes_ref[holder * RM : (holder + 1) * RM, part] = src[40 : 40 + RM, :]
    last = GROUP * GROUP - 1
    big_ref[last : last + 1, :] = jnp.ones((1, IF), f32)
    dir_ref[...] = jnp.concatenate(
        [own_right[48:64, :], own_upper[48:64, :], -left_ref[48:64, :], -lower_ref[48:64, :]], axis=1
    )


def face_values(vectors, place):
    picked = bf_dot(thirds(vectors), place[...])
    return picked[:K] + picked[K : 2 * K] + picked[2 * K :]


def dirichlet_kernel(
    gathered_ref, big_ref, modes_ref, w_ref, faces_ref, double_hbm, single_hbm, hyper_hbm,
    p0, p1, p2, p3, pay_ref,
    double, single, hyper, place, sems,
):
    copies = start_all(((double_hbm, double), (single_hbm, single), (hyper_hbm, hyper)), sems)
    build_places(faces_ref, place)
    coef = first_coefficients(gathered_ref, big_ref)
    w = w_ref[...] + exact_dot(coef, modes_ref[...])
    rounded = bf_dot_nt(w.astype(bf16), place[...])
    rounded_low = rounded.astype(bf16)
    copies[0].wait()
    lifted = (0.5 * rounded + bf_dot(rounded_low, double[...])).astype(bf16)
    copies[1].wait()
    weighed = bf_dot(lifted, single[...]).astype(bf16)
    applied = 0.5 * weighed.astype(f32) + bf_dot_nt(weighed, double[...])
    copies[2].wait()
    applied = applied + bf_dot(rounded_low, hyper[...])
    faces = face_values(applied, place)
    for a, face in enumerate((p0, p1, p2, p3)):
        face[...] = faces[:, a * IF : (a + 1) * IF]
    neighbour_payload(modes_ref, faces, sum_row(rounded * applied), pay_ref)


def neumann_kernel(
    gathered_ref, big_ref, modes_ref, p0, p1, p2, p3, q0, q1, q2, q3, dir_ref, prev_ref, faces_ref, neumann_hbm,
    o0, o1, o2, o3, pay_ref, searched_ref, scale_ref,
    neumann, place, sems,
):
    (copy,) = start_all(((neumann_hbm, neumann),), sems)
    build_places(faces_ref, place)
    coef = coefficients(gathered_ref, big_ref)
    energy = coef[:, SUMS : SUMS + 1]
    eye = lax.broadcasted_iota(jnp.int32, (K, K), 0) == lax.broadcasted_iota(jnp.int32, (K, K), 1)
    prev = jnp.sum(jnp.where(eye, jnp.broadcast_to(prev_ref[...], (K, K)), 0.0), axis=1, keepdims=True)
    ratio = energy / prev
    jumps = jnp.concatenate(
        [p0[...] - q0[...], p1[...] - q1[...], p2[...] - q2[...], p3[...] - q3[...]], axis=1
    )
    searched = jumps + exact_dot(coef, modes_ref[...])
    searched_ref[...] = searched[:, : 2 * IF]
    scale_ref[0] = jnp.broadcast_to(energy, (K, LANES))
    scale_ref[1] = jnp.broadcast_to(ratio, (K, LANES))
    both = jnp.concatenate([searched, dir_ref[...]], axis=0).astype(bf16)
    paired = bf_dot_nt(both, place[...])
    spread_dir = paired[:K] + ratio * paired[K:]
    copy.wait()
    paired_applied = bf_dot(paired.astype(bf16), neumann[...])
    applied_dir = paired_applied[:K] + ratio * paired_applied[K:]
    faces = face_values(applied_dir, place)
    for a, face in enumerate((o0, o1, o2, o3)):
        face[...] = faces[:, a * IF : (a + 1) * IF]
    neighbour_payload(modes_ref, faces, sum_row(spread_dir * applied_dir), pay_ref)


def last_kernel(
    gathered_ref, big_ref, modes_ref, p0, p1, q0, q1, searched_ref, scale_ref, mult_hbm, res_hbm, dir_hbm,
    mult_out, res_out, dir_out,
    mult, res, dirs, sems,
):
    copies = start_all(((mult_hbm, mult), (res_hbm, res), (dir_hbm, dirs)), sems)
    coef = coefficients(gathered_ref, big_ref)
    step = scale_ref[0][:, 0:1] / coef[:, SUMS : SUMS + 1]
    ratio = scale_ref[1][:, 0:1]
    change = exact_dot(coef, modes_ref[:, : 2 * IF])
    for copy in copies:
        copy.wait()
    for s, (p, q) in enumerate(((p0, q0), (p1, q1))):
        part = slice(s * IF, (s + 1) * IF)
        new = searched_ref[:, part] + ratio * dirs[s]
        dir_out[s] = new
        mult_out[s] = mult[s] + step * new
        res_out[s] = res[s] - step * (p[...] - q[...] + change[:, part])


def call(kernel, outs, args, specs=None, scratch=()):
    if specs:
        args = [
            pltpu.with_memory_space_constraint(a, pltpu.HBM) if spec is HBM else a
            for a, spec in zip(args, specs)
        ]
    return pl.pallas_call(
        kernel,
        out_shape=[o if isinstance(o, jax.ShapeDtypeStruct) else jax.ShapeDtypeStruct(o, f32) for o in outs],
        in_specs=specs or [VMEM] * len(args),
        out_specs=[VMEM] * len(outs),
        scratch_shapes=list(scratch),
        compiler_params=pltpu.CompilerParams(vmem_limit_bytes=24 * 2**20),
        name=kernel.__name__,
    )(*args)


def shifted(block, axis, distance):
    devices = range(lax.axis_size(axis))
    route = [((i - distance) % len(devices), i) for i in devices]
    return lax.ppermute(block, axis, route)


def gather_all(copies):
    devices = lax.axis_size("row") * lax.axis_size("col")
    blocks = copies.reshape(devices, -1, LANES)
    return lax.all_to_all(blocks, ("row", "col"), 0, 0).reshape(copies.shape)


def on_device(
    multipliers, residual, direction, energy_prev, hypersingular, double_layer, single_inverse,
    neumann_inverse, rigid_modes, coarse_inverse, face_index,
):
    res, mult, dirs = residual[0], multipliers[0], direction[0]
    dma = pltpu.SemaphoreType.DMA
    res_left = shifted(res, "col", 1)
    res_below = shifted(res, "row", 1)
    rf, faces, to_right, to_upper, to_left, to_lower = call(
        prepare_kernel,
        [(8, NF), jax.ShapeDtypeStruct((4, IF), jnp.int32)] + [(64, IF)] * 4,
        (face_index[0], rigid_modes[0], coarse_inverse, dirs),
        [HBM] * 4,
        [
            pltpu.VMEM((RM, NB), f32), pltpu.VMEM(coarse_inverse.shape, f32), pltpu.VMEM((2, K, IF), f32),
            dma((4,)),
        ],
    )
    w, pay = call(
        first_kernel,
        [(K, NF), (256, LANES)],
        (res, res_left, res_below, rf),
        [HBM] + [VMEM] * 3,
        [pltpu.VMEM((2, K, IF), f32), dma((1,))],
    )
    gathered = gather_all(pay)
    from_left = shifted(to_right, "col", 1)
    from_below = shifted(to_upper, "row", 1)
    from_right = shifted(to_left, "col", -1)
    from_above = shifted(to_lower, "row", -1)
    big, modes, dir_faces = call(
        assemble_kernel,
        [(GROUP * GROUP, 256), (GROUP, NF), (K, NF)],
        (to_right, to_upper, rf, from_right, from_above, from_left, from_below),
    )
    *own, pay = call(
        dirichlet_kernel,
        [(K, IF)] * 4 + [(1024, LANES)],
        (gathered, big, modes, w, faces, double_layer[0], single_inverse[0], hypersingular[0]),
        [VMEM] * 5 + [HBM] * 3,
        [pltpu.VMEM((NB, NB), bf16)] * 3 + [pltpu.VMEM((NB, NF), bf16), dma((3,))],
    )
    gathered = gather_all(pay)
    other = (
        shifted(own[2], "col", -1), shifted(own[3], "row", -1),
        shifted(own[0], "col", 1), shifted(own[1], "row", 1),
    )
    *own, pay, searched, scale = call(
        neumann_kernel,
        [(K, IF)] * 4 + [(1024, LANES), (K, 2 * IF), (2, K, LANES)],
        (
            gathered, big, modes, *own, *other, dir_faces, energy_prev.reshape(1, K), faces,
            neumann_inverse[0],
        ),
        [VMEM] * 14 + [HBM],
        [pltpu.VMEM((NB, NB), bf16), pltpu.VMEM((NB, NF), bf16), dma((1,))],
    )
    gathered = gather_all(pay)
    other = shifted(own[2], "col", -1), shifted(own[3], "row", -1)
    mult_next, res_next, dir_next = call(
        last_kernel,
        [(2, K, IF)] * 3,
        (gathered, big, modes, own[0], own[1], *other, searched, scale, mult, res, dirs),
        [VMEM] * 9 + [HBM] * 3,
        [pltpu.VMEM((2, K, IF), f32)] * 3 + [dma((3,))],
    )
    return mult_next[None], res_next[None], dir_next[None]


def solution(mesh):
    whole = P(("row", "col"), None, None, None)
    patch = P(("row", "col"), None, None)
    return jax.shard_map(
        on_device,
        mesh=mesh,
        in_specs=(whole, whole, whole, P(), patch, patch, patch, patch, patch, P(("row", "col"), None), patch),
        out_specs=(whole, whole, whole),
        check_vma=False,
    )
```

```python
import jax
import jax.numpy as jnp
from jax import lax
from jax.experimental import pallas as pl
from jax.experimental.pallas import tpu as pltpu
from jax.sharding import PartitionSpec as P


NB = 1152
IF = 256
NF = 4 * IF
K = 16
RM = 6
GROUP = 32
SUMS = 31
CELLS = 64
LANES = 128
f32 = jnp.float32
bf16 = jnp.bfloat16
highest = lax.Precision.HIGHEST
fine = lax.Precision.HIGH
contract_last = (((1,), (1,)), ((), ()))
VMEM = pl.BlockSpec(memory_space=pltpu.VMEM)
HBM = pl.BlockSpec(memory_space=pltpu.HBM)


def exact_dot(a, b, precision=highest):
    return jnp.dot(a, b, precision=precision, preferred_element_type=f32)


def exact_dot_nt(a, b, precision=highest):
    return lax.dot_general(a, b, contract_last, precision=precision, preferred_element_type=f32)


def bf_dot(a, b):
    return jnp.dot(a, b, preferred_element_type=f32)


def bf_dot_nt(a, b):
    return lax.dot_general(a, b, contract_last, preferred_element_type=f32)


def thirds(x):
    high = x.astype(bf16).astype(f32)
    rest = x - high
    middle = rest.astype(bf16).astype(f32)
    return jnp.concatenate([high, middle, rest - middle], axis=0).astype(bf16)


def halves(x):
    high = x.astype(bf16).astype(f32)
    return jnp.concatenate([high, x - high], axis=0).astype(bf16)


def joined(x):
    rows = x.shape[0] // 2
    return x[:rows] + x[rows:]


def one_hot(face_ref, a):
    where = face_ref[a : a + 1, :]
    rows = lax.broadcasted_iota(jnp.int32, (NB, IF), 0)
    return jnp.where(rows == where, 1.0, 0.0).astype(bf16)


def build_places(face_ref, place):
    for a in range(4):
        place[:, a * IF : (a + 1) * IF] = one_hot(face_ref, a)


def fold_matrix():
    case = lax.broadcasted_iota(jnp.int32, (K, LANES), 0)
    lane = lax.broadcasted_iota(jnp.int32, (K, LANES), 1)
    return jnp.where((lane & (K - 1)) == case, 1.0, 0.0).astype(f32)


def sum_row(prod):
    row = lax.broadcasted_iota(jnp.int32, (8, prod.shape[1]), 0)
    sums = exact_dot_nt(jnp.where(row == 7, 1.0, 0.0).astype(f32), prod)
    return jnp.concatenate([jnp.zeros((GROUP - 8, K), f32), sums], axis=0)


def flattened(terms):
    rows = terms.shape[0]
    spread_out = exact_dot(terms, fold_matrix())
    row = lax.broadcasted_iota(jnp.int32, (rows, LANES), 0)
    lane = lax.broadcasted_iota(jnp.int32, (rows, LANES), 1)
    kept = jnp.where((lane >> 4) == (row & 7), spread_out, 0.0)
    return jnp.sum(kept.reshape(rows // 8, 8, LANES), axis=1)


def copied(row_block, ref):
    ref[...] = jnp.broadcast_to(row_block[None], (ref.shape[0] // 8, 8, LANES)).reshape(ref.shape)


def fold_terms(terms, blocks, total):
    lane = lax.broadcasted_iota(jnp.int32, (GROUP, LANES), 1)
    for m in range(blocks):
        total = total + jnp.where((lane >> 4) == m, terms[m * GROUP : (m + 1) * GROUP], 0.0)
    return total


def first_coefficients(gathered_ref, coarse_ref):
    terms = exact_dot(coarse_ref[: RM * GROUP], gathered_ref[...], fine)
    return exact_dot_nt(fold_matrix(), fold_terms(terms, RM, jnp.zeros((GROUP, LANES), f32)))


def coefficients(gathered_ref, coarse_ref):
    total = jnp.zeros((GROUP, LANES), f32)
    for q in range(4):
        lanes = gathered_ref[pl.ds(q, 256, stride=4), :]
        total = fold_terms(exact_dot(coarse_ref[q * 256 : (q + 1) * 256], lanes, fine), 8, total)
    return exact_dot_nt(fold_matrix(), total)


def neighbour_payload(modes_ref, faces, sums, pay_ref):
    terms = sums - exact_dot_nt(modes_ref[...], faces, fine)
    flat = flattened(terms)
    copied(jnp.concatenate([flat, flat], axis=0), pay_ref)


def start_all(pairs, sems):
    copies = [pltpu.make_async_copy(src, dst, sems.at[i]) for i, (src, dst) in enumerate(pairs)]
    for copy in copies:
        copy.start()
    return copies


def coarse_by_mode(coarse):
    width = CELLS * RM
    rows = jnp.concatenate([coarse[:, c * width : (c + 1) * width] for c in range(4)], axis=0)
    source = lax.broadcasted_iota(jnp.int32, (width, width), 0)
    target = lax.broadcasted_iota(jnp.int32, (width, width), 1)
    wanted = (target & (CELLS - 1)) * RM + (target >> 6)
    sorting = jnp.where(source == wanted, 1.0, 0.0).astype(bf16)
    moved = bf_dot(thirds(rows), sorting)
    moved = moved[: 4 * RM] + moved[4 * RM : 8 * RM] + moved[8 * RM :]
    return [
        jnp.concatenate(
            [moved[c * RM : (c + 1) * RM, m * CELLS : (m + 1) * CELLS] for c in range(4)], axis=1
        )
        for m in range(RM)
    ]


def prepare_kernel(
    face_hbm, modes_hbm, coarse_hbm, dir_hbm, res_hbm,
    rf_ref, faces_ref, res_ref, right_ref, upper_ref, left_ref, lower_ref,
    modes_in, coarse_in, dir_in, sems,
):
    copies = start_all(
        (
            (face_hbm, faces_ref), (modes_hbm, modes_in), (coarse_hbm, coarse_in), (dir_hbm, dir_in),
            (res_hbm, res_ref),
        ),
        sems,
    )
    for copy in copies:
        copy.wait()
    modes = jnp.concatenate([modes_in[m] for m in range(RM)] + [jnp.zeros((8 - RM, NB), f32)], axis=0)
    parts = thirds(modes)
    sorted_rows = coarse_by_mode(coarse_in[...])
    for a, message in enumerate((right_ref, upper_ref, left_ref, lower_ref)):
        picked = bf_dot(parts, one_hot(faces_ref, a))
        rf = picked[:8] + picked[8:16] + picked[16:24]
        rf_ref[:, a * IF : (a + 1) * IF] = rf
        for m in range(RM):
            message[m * RM : (m + 1) * RM, :] = sorted_rows[m]
        message[36:40, :] = jnp.zeros((4, IF), f32)
        message[40:48, :] = rf
        if a < 2:
            message[48:64, :] = dir_in[a]
            message[64:80, :] = res_ref[a]


def first_kernel(res_ref, left_ref, lower_ref, rf_ref, w_ref, pay_ref):
    w = jnp.concatenate([res_ref[0], res_ref[1], -left_ref[64:80, :], -lower_ref[64:80, :]], axis=1)
    w_ref[...] = w
    flat = flattened(exact_dot_nt(rf_ref[...], w, fine))
    copied(jnp.broadcast_to(flat, (8, LANES)), pay_ref)


def moved_to(rows, p):
    lane = lax.broadcasted_iota(jnp.int32, rows.shape, 1) & 15
    if p == 0:
        return rows
    if p == 1:
        return jnp.where(lane == 15, pltpu.roll(rows, 15, 1), pltpu.roll(rows, 255, 1))
    if p == 2:
        return pltpu.roll(rows, 240, 1)
    if p == 3:
        return jnp.where(lane == 0, pltpu.roll(rows, 241, 1), pltpu.roll(rows, 1, 1))
    return pltpu.roll(rows, 16, 1)


def assemble_kernel(
    own_right, own_upper, rf_ref, right_ref, upper_ref, left_ref, lower_ref, big_ref, modes_ref, dir_ref
):
    big_ref[...] = jnp.zeros_like(big_ref)
    modes_ref[...] = jnp.zeros_like(modes_ref)
    modes_ref[0:RM, :] = -rf_ref[0:RM, :]
    for holder, src in enumerate((own_right, right_ref, upper_ref, left_ref, lower_ref)):
        rows = src[0:40, :]
        for p in range(5):
            moved = moved_to(rows, p)
            for m in range(RM):
                at = (p * RM + m) * GROUP + holder * RM
                big_ref[at : at + RM, :] = moved[m * RM : (m + 1) * RM, :]
        if holder:
            part = slice((holder - 1) * IF, holder * IF)
            modes_ref[holder * RM : (holder + 1) * RM, part] = src[40 : 40 + RM, :]
    last = GROUP * GROUP - 1
    big_ref[last : last + 1, :] = jnp.ones((1, IF), f32)
    dir_ref[...] = jnp.concatenate(
        [own_right[48:64, :], own_upper[48:64, :], -left_ref[48:64, :], -lower_ref[48:64, :]], axis=1
    )


def operator_kernel(
    w_ref, modes_ref, faces_ref, double_hbm, single_hbm, hyper_hbm,
    out_ref,
    double, single, hyper, place, sems,
):
    copies = start_all(((double_hbm, double), (single_hbm, single), (hyper_hbm, hyper)), sems)
    build_places(faces_ref, place)
    parts = halves(jnp.concatenate([w_ref[...], modes_ref[...]], axis=0))
    spread = bf_dot_nt(parts, place[...])
    spread_low = spread.astype(bf16)
    copies[0].wait()
    lifted = halves(joined(0.5 * spread + bf_dot(spread_low, double[...])))
    copies[1].wait()
    weighed = joined(bf_dot(lifted, single[...]))
    applied = 0.5 * weighed + joined(bf_dot_nt(halves(weighed), double[...]))
    copies[2].wait()
    applied = applied + joined(bf_dot(spread_low, hyper[...]))
    out_ref[...] = joined(bf_dot(halves(applied), place[...]))


def dirichlet_kernel(gathered_ref, big_ref, modes_ref, w_ref, applied_ref, p0, p1, p2, p3, pay_ref):
    coef = first_coefficients(gathered_ref, big_ref)
    both = jnp.concatenate([modes_ref[...], applied_ref[K:, :]], axis=1)
    change = exact_dot(coef, both, fine)
    w = w_ref[...] + change[:, :NF]
    faces = applied_ref[:K, :] + change[:, NF:]
    for a, face in enumerate((p0, p1, p2, p3)):
        face[...] = faces[:, a * IF : (a + 1) * IF]
    neighbour_payload(modes_ref, faces, sum_row(w * faces), pay_ref)


def solve_kernel(
    p0, p1, p2, p3, q0, q1, q2, q3, dir_ref, modes_ref, faces_ref, neumann_hbm,
    jump_ref, out_ref,
    neumann, place, sems,
):
    (copy,) = start_all(((neumann_hbm, neumann),), sems)
    build_places(faces_ref, place)
    jumps = jnp.concatenate(
        [p0[...] - q0[...], p1[...] - q1[...], p2[...] - q2[...], p3[...] - q3[...]], axis=1
    )
    jump_ref[...] = jumps
    parts = halves(jnp.concatenate([jumps, dir_ref[...], modes_ref[...]], axis=0))
    spread = bf_dot_nt(parts, place[...]).astype(bf16)
    copy.wait()
    solved = joined(bf_dot(spread, neumann[...]))
    out_ref[...] = joined(bf_dot(halves(solved), place[...]))


def neumann_kernel(
    gathered_ref, big_ref, modes_ref, jump_ref, dir_ref, solved_ref, prev_ref,
    o0, o1, o2, o3, pay_ref, searched_ref, scale_ref,
):
    coef = coefficients(gathered_ref, big_ref)
    energy = coef[:, SUMS : SUMS + 1]
    eye = lax.broadcasted_iota(jnp.int32, (K, K), 0) == lax.broadcasted_iota(jnp.int32, (K, K), 1)
    prev = jnp.sum(jnp.where(eye, jnp.broadcast_to(prev_ref[...], (K, K)), 0.0), axis=1, keepdims=True)
    ratio = energy / prev
    both = jnp.concatenate([modes_ref[...], solved_ref[2 * K :, :]], axis=1)
    change = exact_dot(coef, both, fine)
    searched = jump_ref[...] + change[:, :NF]
    faces = solved_ref[:K, :] + change[:, NF:] + ratio * solved_ref[K : 2 * K, :]
    searched_ref[...] = searched[:, : 2 * IF]
    scale_ref[0] = jnp.broadcast_to(energy, (K, LANES))
    scale_ref[1] = jnp.broadcast_to(ratio, (K, LANES))
    spread_dir = searched + ratio * dir_ref[...]
    for a, face in enumerate((o0, o1, o2, o3)):
        face[...] = faces[:, a * IF : (a + 1) * IF]
    neighbour_payload(modes_ref, faces, sum_row(spread_dir * faces), pay_ref)


def last_kernel(
    gathered_ref, big_ref, modes_ref, p0, p1, q0, q1, searched_ref, scale_ref, mult_hbm, res_hbm, dir_hbm,
    mult_out, res_out, dir_out,
    mult, res, dirs, sems,
):
    copies = start_all(((mult_hbm, mult), (res_hbm, res), (dir_hbm, dirs)), sems)
    coef = coefficients(gathered_ref, big_ref)
    step = scale_ref[0][:, 0:1] / coef[:, SUMS : SUMS + 1]
    ratio = scale_ref[1][:, 0:1]
    change = exact_dot(coef, modes_ref[:, : 2 * IF], fine)
    for copy in copies:
        copy.wait()
    for s, (p, q) in enumerate(((p0, q0), (p1, q1))):
        part = slice(s * IF, (s + 1) * IF)
        new = searched_ref[:, part] + ratio * dirs[s]
        dir_out[s] = new
        mult_out[s] = mult[s] + step * new
        res_out[s] = res[s] - step * (p[...] - q[...] + change[:, part])


def call(kernel, outs, args, specs=None, scratch=()):
    if specs:
        args = [
            pltpu.with_memory_space_constraint(a, pltpu.HBM) if spec is HBM else a
            for a, spec in zip(args, specs)
        ]
    return pl.pallas_call(
        kernel,
        out_shape=[o if isinstance(o, jax.ShapeDtypeStruct) else jax.ShapeDtypeStruct(o, f32) for o in outs],
        in_specs=specs or [VMEM] * len(args),
        out_specs=[VMEM] * len(outs),
        scratch_shapes=list(scratch),
        compiler_params=pltpu.CompilerParams(vmem_limit_bytes=24 * 2**20),
        name=kernel.__name__,
    )(*args)


def shifted(block, axis, distance):
    devices = range(lax.axis_size(axis))
    route = [((i - distance) % len(devices), i) for i in devices]
    return lax.ppermute(block, axis, route)


def gather_all(copies):
    devices = lax.axis_size("row") * lax.axis_size("col")
    blocks = copies.reshape(devices, -1, LANES)
    return lax.all_to_all(blocks, ("row", "col"), 0, 0).reshape(copies.shape)


def on_device(
    multipliers, residual, direction, energy_prev, hypersingular, double_layer, single_inverse,
    neumann_inverse, rigid_modes, coarse_inverse, face_index,
):
    res, mult, dirs = residual[0], multipliers[0], direction[0]
    dma = pltpu.SemaphoreType.DMA
    rf, faces, res_here, to_right, to_upper, to_left, to_lower = call(
        prepare_kernel,
        [(8, NF), jax.ShapeDtypeStruct((4, IF), jnp.int32), (2, K, IF)] + [(80, IF)] * 2 + [(48, IF)] * 2,
        (face_index[0], rigid_modes.transpose(1, 0, 2), coarse_inverse, dirs, res),
        [HBM] * 5,
        [
            pltpu.VMEM((RM, 1, NB), f32), pltpu.VMEM(coarse_inverse.shape, f32), pltpu.VMEM((2, K, IF), f32),
            dma((5,)),
        ],
    )
    from_left = shifted(to_right, "col", 1)
    from_below = shifted(to_upper, "row", 1)
    w, pay = call(first_kernel, [(K, NF), (256, LANES)], (res_here, from_left, from_below, rf))
    gathered = gather_all(pay)
    from_right = shifted(to_left, "col", -1)
    from_above = shifted(to_lower, "row", -1)
    big, modes, dir_faces = call(
        assemble_kernel,
        [(GROUP * GROUP, 256), (GROUP, NF), (K, NF)],
        (to_right, to_upper, rf, from_right, from_above, from_left, from_below),
    )
    (applied,) = call(
        operator_kernel,
        [(K + GROUP, NF)],
        (w, modes, faces, double_layer[0], single_inverse[0], hypersingular[0]),
        [VMEM] * 3 + [HBM] * 3,
        [pltpu.VMEM((NB, NB), bf16)] * 3 + [pltpu.VMEM((NB, NF), bf16), dma((3,))],
    )
    *own, pay = call(
        dirichlet_kernel, [(K, IF)] * 4 + [(1024, LANES)], (gathered, big, modes, w, applied)
    )
    gathered = gather_all(pay)
    other = (
        shifted(own[2], "col", -1), shifted(own[3], "row", -1),
        shifted(own[0], "col", 1), shifted(own[1], "row", 1),
    )
    jump, solved = call(
        solve_kernel,
        [(K, NF), (2 * K + GROUP, NF)],
        (*own, *other, dir_faces, modes, faces, neumann_inverse[0]),
        [VMEM] * 11 + [HBM],
        [pltpu.VMEM((NB, NB), bf16), pltpu.VMEM((NB, NF), bf16), dma((1,))],
    )
    *own, pay, searched, scale = call(
        neumann_kernel,
        [(K, IF)] * 4 + [(1024, LANES), (K, 2 * IF), (2, K, LANES)],
        (gathered, big, modes, jump, dir_faces, solved, energy_prev.reshape(1, K)),
    )
    gathered = gather_all(pay)
    other = shifted(own[2], "col", -1), shifted(own[3], "row", -1)
    mult_next, res_next, dir_next = call(
        last_kernel,
        [(2, K, IF)] * 3,
        (gathered, big, modes, own[0], own[1], *other, searched, scale, mult, res, dirs),
        [VMEM] * 9 + [HBM] * 3,
        [pltpu.VMEM((2, K, IF), f32)] * 3 + [dma((3,))],
    )
    return mult_next[None], res_next[None], dir_next[None]


def solution(mesh):
    whole = P(("row", "col"), None, None, None)
    patch = P(("row", "col"), None, None)
    return jax.shard_map(
        on_device,
        mesh=mesh,
        in_specs=(whole, whole, whole, P(), patch, patch, patch, patch, patch, P(("row", "col"), None), patch),
        out_specs=(whole, whole, whole),
        check_vma=False,
    )
```

```python
import jax
import jax.numpy as jnp
from jax import lax
from jax.experimental import pallas as pl
from jax.experimental.pallas import tpu as pltpu
from jax.sharding import PartitionSpec as P


NB = 1152
IF = 256
NF = 4 * IF
K = 16
RM = 6
GROUP = 32
SUMS = 31
CELLS = 64
LANES = 128
f32 = jnp.float32
bf16 = jnp.bfloat16
highest = lax.Precision.HIGHEST
fine = lax.Precision.HIGH
contract_last = (((1,), (1,)), ((), ()))
VMEM = pl.BlockSpec(memory_space=pltpu.VMEM)
HBM = pl.BlockSpec(memory_space=pltpu.HBM)


def exact_dot(a, b, precision=highest):
    return jnp.dot(a, b, precision=precision, preferred_element_type=f32)


def exact_dot_nt(a, b, precision=highest):
    return lax.dot_general(a, b, contract_last, precision=precision, preferred_element_type=f32)


def bf_dot(a, b):
    return jnp.dot(a, b, preferred_element_type=f32)


def bf_dot_nt(a, b):
    return lax.dot_general(a, b, contract_last, preferred_element_type=f32)


def thirds(x):
    high = x.astype(bf16).astype(f32)
    rest = x - high
    middle = rest.astype(bf16).astype(f32)
    return jnp.concatenate([high, middle, rest - middle], axis=0).astype(bf16)


def halves(x):
    high = x.astype(bf16).astype(f32)
    return jnp.concatenate([high, x - high], axis=0).astype(bf16)


def joined(x):
    rows = x.shape[0] // 2
    return x[:rows] + x[rows:]


def one_hot(face_ref, a):
    where = face_ref[a : a + 1, :]
    rows = lax.broadcasted_iota(jnp.int32, (NB, IF), 0)
    return jnp.where(rows == where, 1.0, 0.0).astype(bf16)


def build_places(face_ref, place):
    for a in range(4):
        place[:, a * IF : (a + 1) * IF] = one_hot(face_ref, a)


def fold_matrix():
    case = lax.broadcasted_iota(jnp.int32, (K, LANES), 0)
    lane = lax.broadcasted_iota(jnp.int32, (K, LANES), 1)
    return jnp.where((lane & (K - 1)) == case, 1.0, 0.0).astype(f32)


def sum_row(prod, at):
    row = lax.broadcasted_iota(jnp.int32, (GROUP, prod.shape[1]), 0)
    return exact_dot_nt(jnp.where(row == at, 1.0, 0.0).astype(f32), prod)


def flattened(terms):
    rows = terms.shape[0]
    spread_out = exact_dot(terms, fold_matrix())
    row = lax.broadcasted_iota(jnp.int32, (rows, LANES), 0)
    lane = lax.broadcasted_iota(jnp.int32, (rows, LANES), 1)
    kept = jnp.where((lane >> 4) == (row & 7), spread_out, 0.0)
    return jnp.sum(kept.reshape(rows // 8, 8, LANES), axis=1)


def copied(row_block, ref):
    ref[...] = jnp.broadcast_to(row_block[None], (ref.shape[0] // 8, 8, LANES)).reshape(ref.shape)


def fold_terms(terms, blocks, total):
    lane = lax.broadcasted_iota(jnp.int32, (GROUP, LANES), 1)
    for m in range(blocks):
        total = total + jnp.where((lane >> 4) == m, terms[m * GROUP : (m + 1) * GROUP], 0.0)
    return total


def first_coefficients(gathered_ref, coarse_ref):
    terms = exact_dot(coarse_ref[: RM * GROUP], gathered_ref[...], fine)
    return exact_dot_nt(fold_matrix(), fold_terms(terms, RM, jnp.zeros((GROUP, LANES), f32)))


def coefficients(gathered_ref, coarse_ref):
    total = jnp.zeros((GROUP, LANES), f32)
    for q in range(4):
        lanes = gathered_ref[pl.ds(q, 256, stride=4), :]
        total = fold_terms(exact_dot(coarse_ref[q * 256 : (q + 1) * 256], lanes, fine), 8, total)
    return exact_dot_nt(fold_matrix(), total)


def column_coefficients(gathered_ref, coarse_ref):
    row = lax.broadcasted_iota(jnp.int32, (GROUP, LANES), 0)
    lane = lax.broadcasted_iota(jnp.int32, (GROUP, LANES), 1)
    total = jnp.zeros((GROUP, LANES), f32)
    for b, p in enumerate((0, 1, 3)):
        lanes = jnp.concatenate([gathered_ref[pl.ds(b * 16 + r, 16, stride=48), :] for r in range(16)], axis=0)
        at = p * RM * GROUP
        total = fold_terms(exact_dot(coarse_ref[at : at + RM * GROUP], lanes, fine), RM, total)
        if b == 0:
            sums = jnp.sum(lanes, axis=0, keepdims=True)
            total = total + jnp.where((row == SUMS) & ((lane >> 4) == RM), sums, 0.0)
    return exact_dot_nt(fold_matrix(), total)


def column_kernel(y_ref, _, out_ref):
    y0, y1, y2, y3 = (y_ref[pl.ds(q, K, stride=4), :] for q in range(4))
    lane = lax.broadcasted_iota(jnp.int32, (K, LANES), 1)
    up = jnp.where(lane < 96, y3, 0.0)
    low = jnp.where(lane < 32, pltpu.roll(y3, 32, 1), jnp.where(lane < 64, pltpu.roll(y1, 64, 1), pltpu.roll(y2, 96, 1)))
    low = jnp.where(lane < 96, low, 0.0)
    own = y0 + pltpu.roll(up, 1, 0) + pltpu.roll(low, 15, 0)
    block = jnp.concatenate([own, y1, y2], axis=0)
    out_ref[...] = jnp.broadcast_to(block[None], (K, 3 * K, LANES)).reshape(out_ref.shape)


def neighbour_payload(modes_ref, faces, sums, pay_ref):
    terms = sums - exact_dot_nt(modes_ref[...], faces, fine)
    flat = flattened(terms)
    copied(jnp.concatenate([flat, flat], axis=0), pay_ref)


def start_all(pairs, sems):
    copies = [pltpu.make_async_copy(src, dst, sems.at[i]) for i, (src, dst) in enumerate(pairs)]
    for copy in copies:
        copy.start()
    return copies


def coarse_by_mode(coarse):
    width = CELLS * RM
    rows = jnp.concatenate([coarse[:, c * width : (c + 1) * width] for c in range(4)], axis=0)
    source = lax.broadcasted_iota(jnp.int32, (width, width), 0)
    target = lax.broadcasted_iota(jnp.int32, (width, width), 1)
    wanted = (target & (CELLS - 1)) * RM + (target >> 6)
    sorting = jnp.where(source == wanted, 1.0, 0.0).astype(bf16)
    moved = bf_dot(thirds(rows), sorting)
    moved = moved[: 4 * RM] + moved[4 * RM : 8 * RM] + moved[8 * RM :]
    return [
        jnp.concatenate(
            [moved[c * RM : (c + 1) * RM, m * CELLS : (m + 1) * CELLS] for c in range(4)], axis=1
        )
        for m in range(RM)
    ]


def prepare_kernel(
    face_hbm, modes_hbm, coarse_hbm, dir_hbm, res_hbm,
    rf_ref, faces_ref, res_ref, right_ref, upper_ref, left_ref, lower_ref,
    modes_in, coarse_in, dir_in, sems,
):
    copies = start_all(
        (
            (face_hbm, faces_ref), (modes_hbm, modes_in), (coarse_hbm, coarse_in), (dir_hbm, dir_in),
            (res_hbm, res_ref),
        ),
        sems,
    )
    for copy in copies:
        copy.wait()
    modes = jnp.concatenate([modes_in[m] for m in range(RM)] + [jnp.zeros((8 - RM, NB), f32)], axis=0)
    parts = thirds(modes)
    sorted_rows = coarse_by_mode(coarse_in[...])
    for a, message in enumerate((right_ref, upper_ref, left_ref, lower_ref)):
        picked = bf_dot(parts, one_hot(faces_ref, a))
        rf = picked[:8] + picked[8:16] + picked[16:24]
        rf_ref[:, a * IF : (a + 1) * IF] = rf
        for m in range(RM):
            message[m * RM : (m + 1) * RM, :] = sorted_rows[m]
        message[36:40, :] = jnp.zeros((4, IF), f32)
        message[40:48, :] = rf
        if a < 2:
            message[48:64, :] = dir_in[a]
            message[64:80, :] = res_ref[a]


def first_kernel(
    res_ref, dir_right, dir_upper, rf_ref, right_ref, upper_ref, left_ref, lower_ref,
    w_ref, dir_ref, modes_ref, column_modes_ref, pay_ref,
):
    w = jnp.concatenate([res_ref[0], res_ref[1], -left_ref[64:80, :], -lower_ref[64:80, :]], axis=1)
    w_ref[...] = w
    flat = flattened(exact_dot_nt(rf_ref[...], w, fine))
    copied(jnp.broadcast_to(flat, (8, LANES)), pay_ref)
    dir_ref[...] = jnp.concatenate(
        [dir_right[48:64, :], dir_upper[48:64, :], -left_ref[48:64, :], -lower_ref[48:64, :]], axis=1
    )
    modes_ref[...] = jnp.zeros_like(modes_ref)
    column_modes_ref[...] = jnp.zeros_like(column_modes_ref)
    modes_ref[0:RM, :] = -rf_ref[0:RM, :]
    column_modes_ref[0:RM, :] = -rf_ref[0:RM, :]
    for p, src in enumerate((right_ref, upper_ref, left_ref)):
        part = slice(p * IF, (p + 1) * IF)
        modes_ref[(p + 1) * RM : (p + 2) * RM, part] = src[40 : 40 + RM, :]
        at = (8, 24, 16)[p]
        column_modes_ref[at : at + RM, part] = src[40 : 40 + RM, :]
    modes_ref[4 * RM : 5 * RM, 3 * IF :] = lower_ref[40 : 40 + RM, :]
    for i, at in ((0, 30), (2, 14), (4, 22)):
        column_modes_ref[at : at + 2, 3 * IF :] = lower_ref[40 + i : 42 + i, :]


def moved_to(rows, p):
    lane = lax.broadcasted_iota(jnp.int32, rows.shape, 1) & 15
    if p == 0:
        return rows
    if p == 1:
        return jnp.where(lane == 15, pltpu.roll(rows, 15, 1), pltpu.roll(rows, 255, 1))
    if p == 2:
        return pltpu.roll(rows, 240, 1)
    if p == 3:
        return jnp.where(lane == 0, pltpu.roll(rows, 241, 1), pltpu.roll(rows, 1, 1))
    return pltpu.roll(rows, 16, 1)


def assemble_kernel(own_ref, right_ref, upper_ref, left_ref, lower_ref, big_ref):
    big_ref[...] = jnp.zeros_like(big_ref)
    for holder, src in enumerate((own_ref, right_ref, upper_ref, left_ref, lower_ref)):
        rows = src[0:40, :]
        for p in range(5):
            moved = moved_to(rows, p)
            for m in range(RM):
                at = (p * RM + m) * GROUP + holder * RM
                big_ref[at : at + RM, :] = moved[m * RM : (m + 1) * RM, :]
    last = GROUP * GROUP - 1
    big_ref[last : last + 1, :] = jnp.ones((1, IF), f32)


def operator_kernel(
    w_ref, modes_ref, faces_ref, double_hbm, single_hbm, hyper_hbm,
    out_ref,
    double, single, hyper, place, sems,
):
    copies = start_all(((double_hbm, double), (single_hbm, single), (hyper_hbm, hyper)), sems)
    build_places(faces_ref, place)
    parts = halves(jnp.concatenate([w_ref[...], modes_ref[...]], axis=0))
    spread = bf_dot_nt(parts, place[...])
    spread_low = spread.astype(bf16)
    copies[0].wait()
    lifted = halves(joined(0.5 * spread + bf_dot(spread_low, double[...])))
    copies[1].wait()
    weighed = joined(bf_dot(lifted, single[...]))
    applied = 0.5 * weighed + joined(bf_dot_nt(halves(weighed), double[...]))
    copies[2].wait()
    applied = applied + joined(bf_dot(spread_low, hyper[...]))
    out_ref[...] = joined(bf_dot(halves(applied), place[...]))


def dirichlet_kernel(gathered_ref, big_ref, modes_ref, w_ref, applied_ref, p0, p1, p2, p3, pay_ref):
    coef = first_coefficients(gathered_ref, big_ref)
    both = jnp.concatenate([modes_ref[...], applied_ref[K:, :]], axis=1)
    change = exact_dot(coef, both, fine)
    w = w_ref[...] + change[:, :NF]
    faces = applied_ref[:K, :] + change[:, NF:]
    for a, face in enumerate((p0, p1, p2, p3)):
        face[...] = faces[:, a * IF : (a + 1) * IF]
    neighbour_payload(modes_ref, faces, sum_row(w * faces, SUMS), pay_ref)


def solve_kernel(
    p0, p1, p2, p3, q0, q1, q2, q3, dir_ref, modes_ref, faces_ref, neumann_hbm,
    jump_ref, out_ref,
    neumann, place, sems,
):
    (copy,) = start_all(((neumann_hbm, neumann),), sems)
    build_places(faces_ref, place)
    jumps = jnp.concatenate(
        [p0[...] - q0[...], p1[...] - q1[...], p2[...] - q2[...], p3[...] - q3[...]], axis=1
    )
    jump_ref[...] = jumps
    parts = halves(jnp.concatenate([jumps, dir_ref[...], modes_ref[...]], axis=0))
    spread = bf_dot_nt(parts, place[...]).astype(bf16)
    copy.wait()
    solved = joined(bf_dot(spread, neumann[...]))
    out_ref[...] = joined(bf_dot(halves(solved), place[...]))


def neumann_kernel(
    gathered_ref, big_ref, modes_ref, column_modes_ref, jump_ref, dir_ref, solved_ref, prev_ref,
    o0, o1, o2, o3, pay_ref, searched_ref, scale_ref,
):
    coef = coefficients(gathered_ref, big_ref)
    energy = coef[:, SUMS : SUMS + 1]
    eye = lax.broadcasted_iota(jnp.int32, (K, K), 0) == lax.broadcasted_iota(jnp.int32, (K, K), 1)
    prev = jnp.sum(jnp.where(eye, jnp.broadcast_to(prev_ref[...], (K, K)), 0.0), axis=1, keepdims=True)
    ratio = energy / prev
    both = jnp.concatenate([modes_ref[...], solved_ref[2 * K :, :]], axis=1)
    change = exact_dot(coef, both, fine)
    searched = jump_ref[...] + change[:, :NF]
    faces = solved_ref[:K, :] + change[:, NF:] + ratio * solved_ref[K : 2 * K, :]
    searched_ref[...] = searched[:, : 2 * IF]
    scale_ref[0] = jnp.broadcast_to(energy, (K, LANES))
    scale_ref[1] = jnp.broadcast_to(ratio, (K, LANES))
    spread_dir = searched + ratio * dir_ref[...]
    for a, face in enumerate((o0, o1, o2, o3)):
        face[...] = faces[:, a * IF : (a + 1) * IF]
    neighbour_payload(column_modes_ref, faces, sum_row(spread_dir * faces, RM), pay_ref)


def last_kernel(
    gathered_ref, big_ref, modes_ref, p0, p1, q0, q1, searched_ref, scale_ref, mult_hbm, res_hbm, dir_hbm,
    mult_out, res_out, dir_out,
    mult, res, dirs, sems,
):
    copies = start_all(((mult_hbm, mult), (res_hbm, res), (dir_hbm, dirs)), sems)
    coef = column_coefficients(gathered_ref, big_ref)
    step = scale_ref[0][:, 0:1] / coef[:, SUMS : SUMS + 1]
    ratio = scale_ref[1][:, 0:1]
    change = exact_dot(coef, modes_ref[:, : 2 * IF], fine)
    for copy in copies:
        copy.wait()
    for s, (p, q) in enumerate(((p0, q0), (p1, q1))):
        part = slice(s * IF, (s + 1) * IF)
        new = searched_ref[:, part] + ratio * dirs[s]
        dir_out[s] = new
        mult_out[s] = mult[s] + step * new
        res_out[s] = res[s] - step * (p[...] - q[...] + change[:, part])


def call(kernel, outs, args, specs=None, scratch=()):
    if specs:
        args = [
            pltpu.with_memory_space_constraint(a, pltpu.HBM) if spec is HBM else a
            for a, spec in zip(args, specs)
        ]
    return pl.pallas_call(
        kernel,
        out_shape=[o if isinstance(o, jax.ShapeDtypeStruct) else jax.ShapeDtypeStruct(o, f32) for o in outs],
        in_specs=specs or [VMEM] * len(args),
        out_specs=[VMEM] * len(outs),
        scratch_shapes=list(scratch),
        compiler_params=pltpu.CompilerParams(vmem_limit_bytes=24 * 2**20),
        name=kernel.__name__,
    )(*args)


def shifted(block, axis, distance):
    devices = range(lax.axis_size(axis))
    route = [((i - distance) % len(devices), i) for i in devices]
    return lax.ppermute(block, axis, route)


def gather_all(copies):
    devices = lax.axis_size("row") * lax.axis_size("col")
    blocks = copies.reshape(devices, -1, LANES)
    return lax.all_to_all(blocks, ("row", "col"), 0, 0).reshape(copies.shape)


def on_device(
    multipliers, residual, direction, energy_prev, hypersingular, double_layer, single_inverse,
    neumann_inverse, rigid_modes, coarse_inverse, face_index,
):
    res, mult, dirs = residual[0], multipliers[0], direction[0]
    dma = pltpu.SemaphoreType.DMA
    rf, faces, res_here, to_right, to_upper, to_left, to_lower = call(
        prepare_kernel,
        [(8, NF), jax.ShapeDtypeStruct((4, IF), jnp.int32), (2, K, IF)] + [(80, IF)] * 2 + [(48, IF)] * 2,
        (face_index[0], rigid_modes.transpose(1, 0, 2), coarse_inverse, dirs, res),
        [HBM] * 5,
        [
            pltpu.VMEM((RM, 1, NB), f32), pltpu.VMEM(coarse_inverse.shape, f32), pltpu.VMEM((2, K, IF), f32),
            dma((5,)),
        ],
    )
    from_left = shifted(to_right, "col", 1)
    from_below = shifted(to_upper, "row", 1)
    from_right = shifted(to_left, "col", -1)
    from_above = shifted(to_lower, "row", -1)
    w, dir_faces, modes, column_modes, pay = call(
        first_kernel,
        [(K, NF), (K, NF), (GROUP, NF), (GROUP, NF), (256, LANES)],
        (res_here, to_right, to_upper, rf, from_right, from_above, from_left, from_below),
    )
    gathered = gather_all(pay)
    (big,) = call(
        assemble_kernel,
        [(GROUP * GROUP, 256)],
        (to_right, from_right, from_above, from_left, from_below),
    )
    (applied,) = call(
        operator_kernel,
        [(K + GROUP, NF)],
        (w, modes, faces, double_layer[0], single_inverse[0], hypersingular[0]),
        [VMEM] * 3 + [HBM] * 3,
        [pltpu.VMEM((NB, NB), bf16)] * 3 + [pltpu.VMEM((NB, NF), bf16), dma((3,))],
    )
    *own, pay = call(
        dirichlet_kernel, [(K, IF)] * 4 + [(1024, LANES)], (gathered, big, modes, w, applied)
    )
    gathered = gather_all(pay)
    other = (
        shifted(own[2], "col", -1), shifted(own[3], "row", -1),
        shifted(own[0], "col", 1), shifted(own[1], "row", 1),
    )
    jump, solved = call(
        solve_kernel,
        [(K, NF), (2 * K + GROUP, NF)],
        (*own, *other, dir_faces, modes, faces, neumann_inverse[0]),
        [VMEM] * 11 + [HBM],
        [pltpu.VMEM((NB, NB), bf16), pltpu.VMEM((NB, NF), bf16), dma((1,))],
    )
    *own, pay, searched, scale = call(
        neumann_kernel,
        [(K, IF)] * 4 + [(64, LANES), (K, 2 * IF), (2, K, LANES)],
        (gathered, big, modes, column_modes, jump, dir_faces, solved, energy_prev.reshape(1, K)),
    )
    column = lax.all_to_all(pay.reshape(K, 4, LANES), "row", 0, 0).reshape(64, LANES)
    from_upper = shifted(own[3], "row", -1)
    (copies,) = call(column_kernel, [(K * 48, LANES)], (column, from_upper))
    gathered = lax.all_to_all(copies.reshape(K, 48, LANES), "col", 0, 0).reshape(K * 48, LANES)
    other = shifted(own[2], "col", -1), from_upper
    mult_next, res_next, dir_next = call(
        last_kernel,
        [(2, K, IF)] * 3,
        (gathered, big, modes, own[0], own[1], *other, searched, scale, mult, res, dirs),
        [VMEM] * 9 + [HBM] * 3,
        [pltpu.VMEM((2, K, IF), f32)] * 3 + [dma((3,))],
    )
    return mult_next[None], res_next[None], dir_next[None]


def solution(mesh):
    whole = P(("row", "col"), None, None, None)
    patch = P(("row", "col"), None, None)
    return jax.shard_map(
        on_device,
        mesh=mesh,
        in_specs=(whole, whole, whole, P(), patch, patch, patch, patch, patch, P(("row", "col"), None), patch),
        out_specs=(whole, whole, whole),
        check_vma=False,
    )
```

```python
import jax
import jax.numpy as jnp
from jax import lax
from jax.experimental import pallas as pl
from jax.experimental.pallas import tpu as pltpu
from jax.sharding import PartitionSpec as P


NB = 1152
IF = 256
NF = 4 * IF
K = 16
RM = 6
GROUP = 32
SUMS = 31
CELLS = 64
LANES = 128
f32 = jnp.float32
bf16 = jnp.bfloat16
highest = lax.Precision.HIGHEST
fine = lax.Precision.HIGH
contract_last = (((1,), (1,)), ((), ()))
VMEM = pl.BlockSpec(memory_space=pltpu.VMEM)
HBM = pl.BlockSpec(memory_space=pltpu.HBM)


def exact_dot(a, b, precision=highest):
    return jnp.dot(a, b, precision=precision, preferred_element_type=f32)


def exact_dot_nt(a, b, precision=highest):
    return lax.dot_general(a, b, contract_last, precision=precision, preferred_element_type=f32)


def bf_dot(a, b):
    return jnp.dot(a, b, preferred_element_type=f32)


def bf_dot_nt(a, b):
    return lax.dot_general(a, b, contract_last, preferred_element_type=f32)


def thirds(x):
    high = x.astype(bf16).astype(f32)
    rest = x - high
    middle = rest.astype(bf16).astype(f32)
    return jnp.concatenate([high, middle, rest - middle], axis=0).astype(bf16)


def halves(x):
    high = x.astype(bf16).astype(f32)
    return jnp.concatenate([high, x - high], axis=0).astype(bf16)


def joined(x):
    rows = x.shape[0] // 2
    return x[:rows] + x[rows:]


def one_hot(face_ref, a):
    where = face_ref[a : a + 1, :]
    rows = lax.broadcasted_iota(jnp.int32, (NB, IF), 0)
    return jnp.where(rows == where, 1.0, 0.0).astype(bf16)


def build_places(face_ref, place):
    for a in range(4):
        place[:, a * IF : (a + 1) * IF] = one_hot(face_ref, a)


def fold_matrix():
    case = lax.broadcasted_iota(jnp.int32, (K, LANES), 0)
    lane = lax.broadcasted_iota(jnp.int32, (K, LANES), 1)
    return jnp.where((lane & (K - 1)) == case, 1.0, 0.0).astype(f32)


def sum_row(prod):
    row = lax.broadcasted_iota(jnp.int32, (8, prod.shape[1]), 0)
    sums = exact_dot_nt(jnp.where(row == 7, 1.0, 0.0).astype(f32), prod)
    return jnp.concatenate([jnp.zeros((GROUP - 8, K), f32), sums], axis=0)


def flattened(terms):
    rows = terms.shape[0]
    spread_out = exact_dot(terms, fold_matrix())
    row = lax.broadcasted_iota(jnp.int32, (rows, LANES), 0)
    lane = lax.broadcasted_iota(jnp.int32, (rows, LANES), 1)
    kept = jnp.where((lane >> 4) == (row & 7), spread_out, 0.0)
    return jnp.sum(kept.reshape(rows // 8, 8, LANES), axis=1)


def copied(row_block, ref):
    ref[...] = jnp.broadcast_to(row_block[None], (ref.shape[0] // 8, 8, LANES)).reshape(ref.shape)


def fold_terms(terms, blocks, total):
    lane = lax.broadcasted_iota(jnp.int32, (GROUP, LANES), 1)
    for m in range(blocks):
        total = total + jnp.where((lane >> 4) == m, terms[m * GROUP : (m + 1) * GROUP], 0.0)
    return total


def first_coefficients(gathered_ref, coarse_ref):
    rows = [gathered_ref[(2 * z + core) * 16 : (2 * z + core + 1) * 16, :] for core in range(2) for z in range(8)]
    terms = exact_dot(coarse_ref[...], jnp.concatenate(rows, axis=0), fine)
    return exact_dot_nt(fold_matrix(), fold_terms(terms, RM, jnp.zeros((GROUP, LANES), f32)))


def partial_kernel(gathered_ref, mine_ref, pair_ref, _, mine_out, pair_out):
    totals = [jnp.zeros((GROUP, LANES), f32)] * 2
    for q in range(4):
        lanes = gathered_ref[pl.ds(q, LANES, stride=4), :]
        part = slice(q * 256, (q + 1) * 256)
        for i, coarse in enumerate((mine_ref, pair_ref)):
            totals[i] = fold_terms(exact_dot(coarse[part, :], lanes, fine), 8, totals[i])
    for out, total in zip((mine_out, pair_out), totals, strict=True):
        out[...] = exact_dot_nt(fold_matrix(), jnp.concatenate([total] * 4, axis=0))


def neighbour_payload(modes_ref, faces, sums, pay_ref):
    terms = sums - exact_dot_nt(modes_ref[...], faces, fine)
    flat = flattened(terms)
    copied(jnp.concatenate([flat, flat], axis=0), pay_ref)


def start_all(pairs, sems):
    copies = [pltpu.make_async_copy(src, dst, sems.at[i]) for i, (src, dst) in enumerate(pairs)]
    for copy in copies:
        copy.start()
    return copies


def coarse_by_mode(coarse):
    width = CELLS * RM
    rows = jnp.concatenate([coarse[:, c * width : (c + 1) * width] for c in range(4)], axis=0)
    source = lax.broadcasted_iota(jnp.int32, (width, width), 0)
    target = lax.broadcasted_iota(jnp.int32, (width, width), 1)
    cell = target & (CELLS - 1)
    patch = ((cell >> 4) & 1) * 32 + (cell >> 5) * 16 + (cell & 15)
    wanted = patch * RM + (target >> 6)
    sorting = jnp.where(source == wanted, 1.0, 0.0).astype(bf16)
    moved = bf_dot(thirds(rows), sorting)
    moved = moved[: 4 * RM] + moved[4 * RM : 8 * RM] + moved[8 * RM :]
    return [
        jnp.concatenate(
            [
                moved[c * RM : (c + 1) * RM, m * CELLS + core * 32 : m * CELLS + (core + 1) * 32]
                for core in range(2)
                for c in range(4)
            ],
            axis=1,
        )
        for m in range(RM)
    ]


def prepare_kernel(
    face_hbm, modes_hbm, coarse_hbm, dir_hbm, res_hbm,
    rf_ref, faces_ref, res_ref, right_ref, upper_ref, left_ref, lower_ref,
    modes_in, coarse_in, dir_in, sems,
):
    copies = start_all(
        (
            (face_hbm, faces_ref), (modes_hbm, modes_in), (coarse_hbm, coarse_in), (dir_hbm, dir_in),
            (res_hbm, res_ref),
        ),
        sems,
    )
    for copy in copies:
        copy.wait()
    modes = jnp.concatenate([modes_in[m] for m in range(RM)] + [jnp.zeros((8 - RM, NB), f32)], axis=0)
    parts = thirds(modes)
    sorted_rows = coarse_by_mode(coarse_in[...])
    for a, message in enumerate((right_ref, upper_ref, left_ref, lower_ref)):
        picked = bf_dot(parts, one_hot(faces_ref, a))
        rf = picked[:8] + picked[8:16] + picked[16:24]
        rf_ref[:, a * IF : (a + 1) * IF] = rf
        for m in range(RM):
            message[m * RM : (m + 1) * RM, :] = sorted_rows[m]
        message[36:40, :] = jnp.zeros((4, IF), f32)
        message[40:48, :] = rf
        if a < 2:
            message[48:64, :] = dir_in[a]
            message[64:80, :] = res_ref[a]


def first_kernel(
    res_ref, dir_right, dir_upper, rf_ref, right_ref, upper_ref, left_ref, lower_ref,
    w_ref, dir_ref, modes_ref, pay_ref,
):
    w = jnp.concatenate([res_ref[0], res_ref[1], -left_ref[64:80, :], -lower_ref[64:80, :]], axis=1)
    w_ref[...] = w
    flat = flattened(exact_dot_nt(rf_ref[...], w, fine))
    copied(jnp.broadcast_to(flat, (8, LANES)), pay_ref)
    dir_ref[...] = jnp.concatenate(
        [dir_right[48:64, :], dir_upper[48:64, :], -left_ref[48:64, :], -lower_ref[48:64, :]], axis=1
    )
    modes_ref[...] = jnp.zeros_like(modes_ref)
    modes_ref[0:RM, :] = -rf_ref[0:RM, :]
    for p, src in enumerate((right_ref, upper_ref, left_ref, lower_ref)):
        modes_ref[(p + 1) * RM : (p + 2) * RM, p * IF : (p + 1) * IF] = src[40 : 40 + RM, :]


def moved_to(rows, p):
    lane = lax.broadcasted_iota(jnp.int32, rows.shape, 1) & 15
    low, high = rows[:, :LANES], rows[:, LANES:]
    if p == 0:
        return rows
    if p == 1:
        return jnp.where(lane == 15, pltpu.roll(rows, 15, 1), pltpu.roll(rows, 255, 1))
    if p == 2:
        return jnp.concatenate([high, pltpu.roll(low, 112, 1)], axis=1)
    if p == 3:
        return jnp.where(lane == 0, pltpu.roll(rows, 241, 1), pltpu.roll(rows, 1, 1))
    return jnp.concatenate([pltpu.roll(high, 16, 1), low], axis=1)


def assemble_kernel(core_ref, own_ref, right_ref, upper_ref, left_ref, lower_ref, first_ref, mine_ref, other_ref):
    for ref in (first_ref, mine_ref, other_ref):
        ref[...] = jnp.zeros_like(ref)
    here = core_ref[0] == 0
    for holder, src in enumerate((own_ref, right_ref, upper_ref, left_ref, lower_ref)):
        rows = src[0:40, :]
        for p in range(5):
            moved = moved_to(rows, p)
            low, high = moved[:, :LANES], moved[:, LANES:]
            mine, other = jnp.where(here, low, high), jnp.where(here, high, low)
            for m in range(RM):
                at, part = (p * RM + m) * GROUP + holder * RM, slice(m * RM, (m + 1) * RM)
                mine_ref[at : at + RM, :] = mine[part]
                other_ref[at : at + RM, :] = other[part]
                if p == 0:
                    first_ref[at : at + RM, :] = moved[part]
    last = GROUP * GROUP - 1
    mine_ref[last : last + 1, :] = jnp.ones((1, LANES), f32)
    other_ref[last : last + 1, :] = jnp.ones((1, LANES), f32)


def operator_kernel(
    w_ref, modes_ref, faces_ref, double_hbm, single_hbm, hyper_hbm,
    out_ref,
    double, single, hyper, place, sems,
):
    copies = start_all(((double_hbm, double), (single_hbm, single), (hyper_hbm, hyper)), sems)
    build_places(faces_ref, place)
    parts = halves(jnp.concatenate([w_ref[...], modes_ref[...]], axis=0))
    spread = bf_dot_nt(parts, place[...])
    spread_low = spread.astype(bf16)
    copies[0].wait()
    lifted = halves(joined(0.5 * spread + bf_dot(spread_low, double[...])))
    copies[1].wait()
    weighed = joined(bf_dot(lifted, single[...]))
    applied = 0.5 * weighed + joined(bf_dot_nt(halves(weighed), double[...]))
    copies[2].wait()
    applied = applied + joined(bf_dot(spread_low, hyper[...]))
    out_ref[...] = joined(bf_dot(halves(applied), place[...]))


def dirichlet_kernel(gathered_ref, big_ref, modes_ref, w_ref, applied_ref, p0, p1, p2, p3, pay_ref):
    coef = first_coefficients(gathered_ref, big_ref)
    both = jnp.concatenate([modes_ref[...], applied_ref[K:, :]], axis=1)
    change = exact_dot(coef, both, fine)
    w = w_ref[...] + change[:, :NF]
    faces = applied_ref[:K, :] + change[:, NF:]
    for a, face in enumerate((p0, p1, p2, p3)):
        face[...] = faces[:, a * IF : (a + 1) * IF]
    neighbour_payload(modes_ref, faces, sum_row(w * faces), pay_ref)


def solve_kernel(
    p0, p1, p2, p3, q0, q1, q2, q3, dir_ref, modes_ref, faces_ref, neumann_hbm,
    jump_ref, out_ref,
    neumann, place, sems,
):
    (copy,) = start_all(((neumann_hbm, neumann),), sems)
    build_places(faces_ref, place)
    jumps = jnp.concatenate(
        [p0[...] - q0[...], p1[...] - q1[...], p2[...] - q2[...], p3[...] - q3[...]], axis=1
    )
    jump_ref[...] = jumps
    parts = halves(jnp.concatenate([jumps, dir_ref[...], modes_ref[...]], axis=0))
    spread = bf_dot_nt(parts, place[...]).astype(bf16)
    copy.wait()
    solved = joined(bf_dot(spread, neumann[...]))
    out_ref[...] = joined(bf_dot(halves(solved), place[...]))


def neumann_kernel(
    mine_ref, pair_ref, modes_ref, jump_ref, dir_ref, solved_ref, prev_ref,
    o0, o1, o2, o3, pay_ref, searched_ref, scale_ref,
):
    coef = (mine_ref[...] + pair_ref[...])[:, :GROUP]
    energy = coef[:, SUMS : SUMS + 1]
    eye = lax.broadcasted_iota(jnp.int32, (K, K), 0) == lax.broadcasted_iota(jnp.int32, (K, K), 1)
    prev = jnp.sum(jnp.where(eye, jnp.broadcast_to(prev_ref[...], (K, K)), 0.0), axis=1, keepdims=True)
    ratio = energy / prev
    both = jnp.concatenate([modes_ref[...], solved_ref[2 * K :, :]], axis=1)
    change = exact_dot(coef, both, fine)
    searched = jump_ref[...] + change[:, :NF]
    faces = solved_ref[:K, :] + change[:, NF:] + ratio * solved_ref[K : 2 * K, :]
    searched_ref[...] = searched[:, : 2 * IF]
    scale_ref[0] = jnp.broadcast_to(energy, (K, LANES))
    scale_ref[1] = jnp.broadcast_to(ratio, (K, LANES))
    spread_dir = searched + ratio * dir_ref[...]
    for a, face in enumerate((o0, o1, o2, o3)):
        face[...] = faces[:, a * IF : (a + 1) * IF]
    neighbour_payload(modes_ref, faces, sum_row(spread_dir * faces), pay_ref)


def last_kernel(
    mine_ref, pair_ref, modes_ref, p0, p1, q0, q1, searched_ref, scale_ref, mult_hbm, res_hbm, dir_hbm,
    mult_out, res_out, dir_out,
    mult, res, dirs, sems,
):
    copies = start_all(((mult_hbm, mult), (res_hbm, res), (dir_hbm, dirs)), sems)
    coef = (mine_ref[...] + pair_ref[...])[:, :GROUP]
    step = scale_ref[0][:, 0:1] / coef[:, SUMS : SUMS + 1]
    ratio = scale_ref[1][:, 0:1]
    change = exact_dot(coef, modes_ref[:, : 2 * IF], fine)
    for copy in copies:
        copy.wait()
    for s, (p, q) in enumerate(((p0, q0), (p1, q1))):
        part = slice(s * IF, (s + 1) * IF)
        new = searched_ref[:, part] + ratio * dirs[s]
        dir_out[s] = new
        mult_out[s] = mult[s] + step * new
        res_out[s] = res[s] - step * (p[...] - q[...] + change[:, part])


def call(kernel, outs, args, specs=None, scratch=()):
    if specs:
        args = [
            pltpu.with_memory_space_constraint(a, pltpu.HBM) if spec is HBM else a
            for a, spec in zip(args, specs)
        ]
    return pl.pallas_call(
        kernel,
        out_shape=[o if isinstance(o, jax.ShapeDtypeStruct) else jax.ShapeDtypeStruct(o, f32) for o in outs],
        in_specs=specs or [VMEM] * len(args),
        out_specs=[VMEM] * len(outs),
        scratch_shapes=list(scratch),
        compiler_params=pltpu.CompilerParams(vmem_limit_bytes=24 * 2**20),
        name=kernel.__name__,
    )(*args)


def shifted(block, axis, distance):
    devices = range(lax.axis_size(axis))
    route = [((i - distance) % len(devices), i) for i in devices]
    return lax.ppermute(block, axis, route)


def gather_all(copies):
    blocks = copies.reshape(256, -1, LANES)
    return lax.all_to_all(blocks, ("row", "col"), 0, 0).reshape(copies.shape)


def across(block):
    return lax.ppermute(block, "row", [(i ^ 1, i) for i in range(lax.axis_size("row"))])


def gather_core(copies):
    groups = [[row * 16 + col for row in range(core, 16, 2) for col in range(16)] for core in range(2)]
    blocks = copies.reshape(128, 4, LANES)
    return lax.all_to_all(blocks, ("row", "col"), 0, 0, axis_index_groups=groups).reshape(copies.shape)


def sums_of(gathered, mine, pair, ready):
    specs = [VMEM] * 3 + [pl.BlockSpec(memory_space=pl.ANY)]
    here, there = call(partial_kernel, [(K, LANES)] * 2, (gathered, mine, pair, ready), specs)
    return here, across(there)


def on_device(
    multipliers, residual, direction, energy_prev, hypersingular, double_layer, single_inverse,
    neumann_inverse, rigid_modes, coarse_inverse, face_index,
):
    res, mult, dirs = residual[0], multipliers[0], direction[0]
    dma = pltpu.SemaphoreType.DMA
    rf, faces, res_here, to_right, to_upper, to_left, to_lower = call(
        prepare_kernel,
        [(8, NF), jax.ShapeDtypeStruct((4, IF), jnp.int32), (2, K, IF)] + [(80, IF)] * 2 + [(48, IF)] * 2,
        (face_index[0], rigid_modes.transpose(1, 0, 2), coarse_inverse, dirs, res),
        [HBM] * 5,
        [
            pltpu.VMEM((RM, 1, NB), f32), pltpu.VMEM(coarse_inverse.shape, f32), pltpu.VMEM((2, K, IF), f32),
            dma((5,)),
        ],
    )
    from_left = shifted(to_right, "col", 1)
    from_below = shifted(to_upper, "row", 1)
    from_right = shifted(to_left, "col", -1)
    from_above = shifted(to_lower, "row", -1)
    w, dir_faces, modes, pay = call(
        first_kernel,
        [(K, NF), (K, NF), (GROUP, NF), (256, LANES)],
        (res_here, to_right, to_upper, rf, from_right, from_above, from_left, from_below),
    )
    gathered = gather_all(pay)
    core = (lax.axis_index("row") & 1).astype(jnp.int32).reshape(1)
    first, mine, other = call(
        assemble_kernel,
        [(RM * GROUP, 256), (GROUP * GROUP, LANES), (GROUP * GROUP, LANES)],
        (core, to_right, from_right, from_above, from_left, from_below),
        [pl.BlockSpec(memory_space=pltpu.SMEM)] + [VMEM] * 5,
    )
    pair = across(other)
    (applied,) = call(
        operator_kernel,
        [(K + GROUP, NF)],
        (w, modes, faces, double_layer[0], single_inverse[0], hypersingular[0]),
        [VMEM] * 3 + [HBM] * 3,
        [pltpu.VMEM((NB, NB), bf16)] * 3 + [pltpu.VMEM((NB, NF), bf16), dma((3,))],
    )
    *own, pay = call(
        dirichlet_kernel, [(K, IF)] * 4 + [(512, LANES)], (gathered, first, modes, w, applied)
    )
    gathered = gather_core(pay)
    other = (
        shifted(own[2], "col", -1), shifted(own[3], "row", -1),
        shifted(own[0], "col", 1), shifted(own[1], "row", 1),
    )
    jump, solved = call(
        solve_kernel,
        [(K, NF), (2 * K + GROUP, NF)],
        (*own, *other, dir_faces, modes, faces, neumann_inverse[0]),
        [VMEM] * 11 + [HBM],
        [pltpu.VMEM((NB, NB), bf16), pltpu.VMEM((NB, NF), bf16), dma((1,))],
    )
    sums = sums_of(gathered, mine, pair, jump)
    *own, pay, searched, scale = call(
        neumann_kernel,
        [(K, IF)] * 4 + [(512, LANES), (K, 2 * IF), (2, K, LANES)],
        (*sums, modes, jump, dir_faces, solved, energy_prev.reshape(1, K)),
    )
    gathered = gather_core(pay)
    other = shifted(own[2], "col", -1), shifted(own[3], "row", -1)
    sums = sums_of(gathered, mine, pair, other[0])
    mult_next, res_next, dir_next = call(
        last_kernel,
        [(2, K, IF)] * 3,
        (*sums, modes, own[0], own[1], *other, searched, scale, mult, res, dirs),
        [VMEM] * 9 + [HBM] * 3,
        [pltpu.VMEM((2, K, IF), f32)] * 3 + [dma((3,))],
    )
    return mult_next[None], res_next[None], dir_next[None]


def solution(mesh):
    whole = P(("row", "col"), None, None, None)
    patch = P(("row", "col"), None, None)
    return jax.shard_map(
        on_device,
        mesh=mesh,
        in_specs=(whole, whole, whole, P(), patch, patch, patch, patch, patch, P(("row", "col"), None), patch),
        out_specs=(whole, whole, whole),
        check_vma=False,
    )
```
